512 devices in a mesh: rows: 128 (over z, x, core), cls: 4 (over y).
Axes of the slice: x: 4, y: 4, z: 16, core: 2. Of those that a mesh axis runs over, the one named last changes fastest.
Arguments:
- centers: bfloat16 [32768, 1280], P('rows', 'cls'), may hold values from 0 to 4
- coefficients: float32 [1000, 32768], P('cls', 'rows'), may hold values from -0.6 to 0.6
- batch_features: bfloat16 [1024, 1280], P('rows', 'cls'), may hold values from 0 to 4
- batch_labels: int32 [1024], replicated, may hold values from 0 to 999
- batch_index: int32 [1024], replicated, may hold values from 0 to 32767
- subset_index: int32 [8192], P('rows'), may hold values from 0 to 32767, as said below
- eigen_vectors: float32 [8192, 512], P('rows'), may hold values from -0.0625 to 0.0625
- eigen_scale: float32 [512], replicated, may hold values from 0.2 to 2
Outputs:
- predicted: float32 [1000, 1024], P('cls')
- new_coefficients: float32 [1000, 32768], P('cls', 'rows')
The draws below stay inside these ranges and needn't reach their ends.
Inputs may be any that keep to these rules, and one draw needn't show every extreme that they name: `subset_index`: entry s lies among the centers (s // 64) * 256 to (s // 64 + 1) * 256 - 1; entry 0 is 0 and the last is 32767.
All inputs are finite; a program needn't handle non-finite values.
Results may differ from the reference program's by a relative error of at most 0.0003.
Values may be sent and summed in bfloat16 or wider, within the bound.
No kernel may reach another device: no remote copies, remote signals or barrier semaphores. Data moves between devices by JAX's collectives and lax.ppermute only.
A program may use at most 64 MiB of HBM per device.

```python
import math
import jax
import jax.numpy as jnp
from jax import lax

D = 1280
C = 1000
Q = 512
B = 1024
CEN_DEV = 256
S_DEV = 64
M = 32768
S = 8192
N_ROWS = 128


cluster_count = 16


def column_scales(key):
    return jnp.exp(jax.random.uniform(jax.random.fold_in(key, 11), (D,), jnp.float32, jnp.log(0.05), jnp.log(0.5)))


def cluster_means(key):
    return 1.2 * jax.random.normal(jax.random.fold_in(key, 13), (cluster_count, D), jnp.float32)


def scaled_features(key, count, salt):
    noise_key = jax.random.fold_in(key, salt)
    scale_key = jax.random.fold_in(key, salt + 1)
    member_key = jax.random.fold_in(key, salt + 2)
    members = jax.random.randint(member_key, (count,), 0, cluster_count, dtype=jnp.int32)
    centre = cluster_means(key)[members]
    noise_part = 0.6 * jnp.clip(jax.random.normal(noise_key, (count, D), jnp.float32), -4.0, 4.0)
    row_scale = jnp.exp(jax.random.uniform(scale_key, (count,), jnp.float32, jnp.log(0.5), jnp.log(2.0)))
    base = centre + noise_part
    scaled = jnp.maximum(base, 0.0) * row_scale[:, None] * column_scales(key)[None, :]
    return jnp.minimum(scaled, 4.0)


def draw_centers(key, part):
    return scaled_features(key, M, 21).astype(jnp.bfloat16)


def draw_batch_features(key, part):
    return scaled_features(key, B, 31).astype(jnp.bfloat16)


def draw_subset_index(key, part):
    positions = jnp.arange(S, dtype=jnp.int32)
    offsets = jax.random.randint(jax.random.fold_in(key, 41), (S,), 0, CEN_DEV, dtype=jnp.int32)
    chosen = positions // S_DEV * CEN_DEV + offsets
    chosen = chosen.at[0].set(0)
    return chosen.at[S - 1].set(M - 1)


def touch_ends(array, rng, least, high):
    longest = array.shape.index(max(array.shape))
    spots = []
    for shift in (0, 1):
        where = [jax.random.randint(jax.random.fold_in(rng, axis), (), 0, length) for axis, length in enumerate(array.shape)]
        where[longest] = (where[longest] + shift) % array.shape[longest]
        spots.append(tuple(where))
    return array.at[spots[0]].set(least).at[spots[1]].set(high)


def block_scale(stream_key, dims, cuts, least, largest):
    gain, own = 1.0, jax.random.fold_in(stream_key, 6)
    for dim, shards_of in cuts:
        steps = jnp.exp(jax.random.uniform(jax.random.fold_in(own, dim), (shards_of,), jnp.float32, least / len(cuts), largest / len(cuts)))
        gain = gain * jnp.repeat(steps, dims[dim] // shards_of).reshape([-1 if axis == dim else 1 for axis in range(len(dims))])
    return gain


def gaussian(key, shape, width, reach, cuts=(), kind=jnp.bfloat16):
    array = jax.random.normal(key, shape, jnp.float32) * width
    if len(cuts) > 0:
        array = block_scale(key, shape, cuts, -0.22, 0.18) * array
    return jnp.clip(array, min=-reach, max=reach).astype(kind)


def setup_inputs(seed: int = 0) -> dict:
    key_list = jax.random.split(jax.random.key(seed), 9)
    return {
        "centers": draw_centers(jax.random.fold_in(key_list[8], 71), 0),
        "coefficients": gaussian(key_list[1], (C, M), 0.1, 0.6, ((0, 4), (1, 128)), jnp.float32),
        "batch_features": draw_batch_features(jax.random.fold_in(key_list[8], 71), 0),
        "batch_labels": touch_ends(jax.random.randint(key_list[3], (B,), 0, C), jax.random.fold_in(key_list[3], 1), 0, C - 1).astype(jnp.int32),
        "batch_index": touch_ends(jax.random.randint(key_list[4], (B,), 0, M), jax.random.fold_in(key_list[4], 1), 0, M - 1).astype(jnp.int32),
        "subset_index": draw_subset_index(jax.random.fold_in(key_list[8], 71), 0),
        "eigen_vectors": gaussian(key_list[6], (S, Q), S ** -0.5, 0.0625, ((0, 128),), jnp.float32),
        "eigen_scale": jnp.clip(jnp.exp(jax.random.uniform(key_list[7], (Q,), jnp.float32, math.log(0.2), math.log(2.0))), 0.2, 2.0),
    }


spread = 4.0
step_rate = 0.5

def kernel_block(inner, row_norm, col_norm):
    squared = row_norm[:, None] + col_norm[None, :] - 2.0 * inner
    return jnp.exp(-jnp.sqrt(jnp.maximum(squared, 0.0)) / spread)

def square_norm(features):
    return lax.optimization_barrier(jnp.sum(jnp.square(features.astype(jnp.float32)), axis=1))

def reference(centers, coefficients, batch_features, batch_labels, batch_index, subset_index, eigen_vectors, eigen_scale):
    batch_norm = square_norm(batch_features)
    center_blocks = centers.reshape(N_ROWS, CEN_DEV, D)
    coef_blocks = jnp.transpose(coefficients.reshape(C, N_ROWS, CEN_DEV), (1, 0, 2))

    def accumulate(totals, blocks_pair):
        center_rows, coef_rows = blocks_pair
        inner = jnp.dot(center_rows, batch_features.T, preferred_element_type=jnp.float32)
        kernel_rows = kernel_block(inner, square_norm(center_rows), batch_norm)
        return (totals + jnp.dot(coef_rows, kernel_rows, precision=lax.Precision.HIGHEST), None)
    predicted = lax.scan(accumulate, jnp.zeros((C, B), jnp.float32), (center_blocks, coef_blocks))[0]
    targets = (batch_labels[None, :] == jnp.arange(C, dtype=jnp.int32)[:, None]).astype(jnp.float32)
    gradient = predicted - targets
    subset_rows = centers[subset_index]
    subset_inner = jnp.dot(subset_rows, batch_features.T, preferred_element_type=jnp.float32)
    subset_kernel = kernel_block(subset_inner, square_norm(subset_rows), batch_norm)
    subset_err = jnp.dot(gradient, subset_kernel.T, precision=lax.Precision.HIGHEST)
    projected = jnp.dot(subset_err, eigen_vectors, precision=lax.Precision.HIGHEST)
    correction = jnp.dot(projected * eigen_scale[None, :], eigen_vectors.T, precision=lax.Precision.HIGHEST)
    updated = coefficients.at[:, batch_index].add(-step_rate * gradient)
    updated = updated.at[:, subset_index].add(step_rate * correction)
    return (predicted, updated)
```

```python
import functools

import jax
import jax.numpy as jnp
from jax import lax
from jax.experimental import pallas as pl
from jax.experimental.pallas import tpu as pltpu
from jax.sharding import Mesh
from jax.sharding import PartitionSpec as P

Z, X, K, Y = "rows_z", "rows_x", "rows_k", "cls"
ROWS = (Z, X, K)
LANES = 128
INTERPRET = False

spread = 4.0
step_rate = 0.5

HIGHEST = lax.Precision.HIGHEST
LAST = (((1,), (1,)), ((), ()))
FIRST = (((0,), (0,)), ((), ()))


def gathered(value, axis):
    copies = jnp.broadcast_to(value, (lax.axis_size(axis), *value.shape))
    return lax.all_to_all(copies, axis, 0, 0, tiled=True)


def scattered(tiles, axis):
    return jnp.sum(lax.all_to_all(tiles, axis, 0, 0, tiled=True), axis=0)


def kernel_products(
    place, batch, centers, coefficients, basis, sums, norms, *, classes, padded, split
):
    block = pl.program_id(0)
    cores, chips, _, depth, rows, width = batch.shape
    groups = centers.shape[0]
    count = centers.shape[1]

    @pl.when(block == 0)
    def _():
        total = jnp.zeros((count, 1), jnp.float32)
        for y in range(groups):
            own = centers[y].astype(jnp.float32)
            total += jnp.sum(own * own, axis=1, keepdims=True)
        norms[...] = jnp.broadcast_to(total, norms.shape)
        for b in range(sums.shape[0]):
            sums[b, classes:padded, :] = jnp.zeros((padded - classes, LANES), jnp.float32)

    inner = jnp.zeros((count, LANES), jnp.float32)
    squares = jnp.zeros((8, LANES), jnp.float32)
    ones = jnp.ones((8, width), jnp.float32)
    for y in range(groups):
        pieces = [
            batch[k, x, y, z]
            for z in range(depth)
            for x in range(chips)
            for k in range(cores)
        ]
        lines = jnp.concatenate(pieces, axis=0)
        inner += lax.dot_general(centers[y], lines, LAST, preferred_element_type=jnp.float32)
        wide = lines.astype(jnp.float32)
        squares += lax.dot_general(
            ones, wide * wide, LAST, precision=HIGHEST, preferred_element_type=jnp.float32
        )
    squared = norms[...] + squares[:1] - 2.0 * inner
    values = jnp.exp(-jnp.sqrt(jnp.maximum(squared, 0.0)) / spread)
    outputs = jnp.dot(
        coefficients[...], values, precision=HIGHEST, preferred_element_type=jnp.float32
    )
    sums[pl.ds(block, 1), :classes, :] = outputs[None]
    own = basis[...].reshape(-1, count)
    part = jnp.dot(own, values, precision=HIGHEST, preferred_element_type=jnp.float32)
    start = pl.multiple_of(padded + block * split, 8)
    sums[:, pl.ds(start, split), :] = part.reshape(-1, split, LANES)


def project(place, predicted, basis, labels, projected, *, classes):
    block = pl.program_id(0)
    rows = predicted.shape[1]
    ids = lax.broadcasted_iota(jnp.int32, (rows, LANES), 0) + place[0] * classes
    gradient = predicted[0] - (labels[0] == ids).astype(jnp.float32)
    own = basis[...].reshape(-1, LANES)
    part = lax.dot_general(
        own, gradient, LAST, precision=HIGHEST, preferred_element_type=jnp.float32
    )

    @pl.when(block == 0)
    def _():
        projected[...] = part

    @pl.when(block > 0)
    def _():
        projected[...] += part


def step_batch(place, predicted, labels, index, coefficients, output, updated, *, classes):
    block = pl.program_id(0)
    rows = predicted.shape[1]
    count = coefficients.shape[1]
    ids = lax.broadcasted_iota(jnp.int32, (rows, LANES), 0) + place[0] * classes
    gradient = predicted[0] - (labels[0] == ids).astype(jnp.float32)
    output[...] = predicted[0, :classes]
    slots = lax.broadcasted_iota(jnp.int32, (count, LANES), 0) + place[1] * count
    hits = (index[0] == slots).astype(jnp.float32)
    part = lax.dot_general(
        gradient, hits, LAST, precision=HIGHEST, preferred_element_type=jnp.float32
    )

    @pl.when(block == 0)
    def _():
        updated[...] = coefficients[...] - step_rate * part[:classes]

    @pl.when(block > 0)
    def _():
        updated[...] += -step_rate * part[:classes]


def correct(updated, projected, weights, result):
    classes = updated.shape[0]
    change = lax.dot_general(
        projected[...], weights[...], FIRST, precision=HIGHEST, preferred_element_type=jnp.float32
    )
    result[...] = updated[...] + change[:classes]


def shards(
    centers,
    coefficients,
    batch_features,
    batch_labels,
    batch_index,
    subset_index,
    eigen_vectors,
    eigen_scale,
):
    depth, chips, cores, groups = (lax.axis_size(a) for a in (Z, X, K, Y))
    blocks = chips * cores
    count = centers.shape[0]
    classes = coefficients.shape[0]
    rank = lax.axis_index(ROWS)
    place = jnp.stack([lax.axis_index(Y), rank]).astype(jnp.int32)
    vectors = eigen_vectors.shape[1]
    split = vectors // groups // blocks
    padded = -(-classes // 8) * 8
    while (padded + vectors // groups) % (8 * depth):
        padded += 8
    lines = padded + vectors // groups
    batch = blocks * LANES
    near = depth // blocks

    centers_all = gathered(centers, Y)
    batch_all = batch_features
    for axis in (Z, Y, X, K):
        batch_all = gathered(batch_all, axis)

    spots = jnp.arange(count, dtype=jnp.int32) + rank * count
    chosen = (subset_index[:, None] == spots[None, :]).astype(jnp.float32)
    lifted = lax.dot_general(eigen_vectors, chosen, FIRST, precision=HIGHEST)
    weights = lifted * (step_rate * eigen_scale)[:, None]
    labels = batch_labels.reshape(blocks, 1, LANES)
    index = batch_index.reshape(blocks, 1, LANES)

    whole = lambda shape: pl.BlockSpec(shape, lambda j, p: (0,) * len(shape))
    sums = pl.pallas_call(
        functools.partial(kernel_products, classes=classes, padded=padded, split=split),
        out_shape=jax.ShapeDtypeStruct((blocks, lines, LANES), jnp.float32),
        grid_spec=pltpu.PrefetchScalarGridSpec(
            num_scalar_prefetch=1,
            grid=(blocks,),
            in_specs=[
                pl.BlockSpec(
                    (cores, chips, groups, near, *batch_features.shape),
                    lambda j, p: (0, 0, 0, j, 0, 0),
                ),
                whole(centers_all.shape),
                whole(coefficients.shape),
                pl.BlockSpec(
                    (blocks, None, split, count), lambda j, p: (0, p[0], 0, 0)
                ),
            ],
            out_specs=whole((blocks, lines, LANES)),
            scratch_shapes=[pltpu.VMEM((count, LANES), jnp.float32)],
        ),
        interpret=INTERPRET,
        name="kernel_products",
    )(
        place,
        batch_all,
        centers_all,
        coefficients,
        lifted.reshape(blocks, groups, split, count),
    )

    own = scattered(sums.reshape(cores, chips, lines, LANES), K)
    own = scattered(own, X)
    own = scattered(own.reshape(depth, lines // depth, LANES), Z)
    own = gathered(own, Z).reshape(lines, LANES)
    basis = gathered(own[padded:].reshape(blocks, split, LANES), Y)
    predicted = gathered(gathered(own[:padded], X), K).reshape(blocks, padded, LANES)

    part = pl.pallas_call(
        functools.partial(project, classes=classes),
        out_shape=jax.ShapeDtypeStruct((groups * split, padded), jnp.float32),
        grid_spec=pltpu.PrefetchScalarGridSpec(
            num_scalar_prefetch=1,
            grid=(blocks,),
            in_specs=[
                pl.BlockSpec((1, padded, LANES), lambda j, p: (j, 0, 0)),
                pl.BlockSpec((groups, None, split, LANES), lambda j, p: (0, j, 0, 0)),
                pl.BlockSpec((1, 1, LANES), lambda j, p: (j, 0, 0)),
            ],
            out_specs=whole((groups * split, padded)),
        ),
        interpret=INTERPRET,
        name="project",
    )(place, predicted, basis, labels)
    projected = gathered(gathered(part, X), K).reshape(vectors, padded)

    output, updated = pl.pallas_call(
        functools.partial(step_batch, classes=classes),
        out_shape=(
            jax.ShapeDtypeStruct((classes, batch), jnp.float32),
            jax.ShapeDtypeStruct((classes, count), jnp.float32),
        ),
        grid_spec=pltpu.PrefetchScalarGridSpec(
            num_scalar_prefetch=1,
            grid=(blocks,),
            in_specs=[
                pl.BlockSpec((1, padded, LANES), lambda j, p: (j, 0, 0)),
                pl.BlockSpec((1, 1, LANES), lambda j, p: (j, 0, 0)),
                pl.BlockSpec((1, 1, LANES), lambda j, p: (j, 0, 0)),
                whole(coefficients.shape),
            ],
            out_specs=(
                pl.BlockSpec((classes, LANES), lambda j, p: (0, j)),
                whole((classes, count)),
            ),
        ),
        interpret=INTERPRET,
        name="step_batch",
    )(place, predicted, labels, index, coefficients)

    result = pl.pallas_call(
        correct,
        out_shape=jax.ShapeDtypeStruct((classes, count), jnp.float32),
        interpret=INTERPRET,
        name="correct",
    )(updated, projected, weights)
    return (output, result)


def solution(mesh, shape=(16, 4, 2)):
    finer = Mesh(mesh.devices.reshape(*shape, mesh.shape["cls"]), (*ROWS, Y))
    placed = (P(ROWS, Y), P(Y, ROWS), P(ROWS, Y), P(), P(), P(ROWS), P(ROWS, None), P())
    return jax.shard_map(
        shards,
        mesh=finer,
        in_specs=placed,
        out_specs=(P(Y, None), P(Y, ROWS)),
        check_vma=False,
    )
```

```python
import functools

import jax
import jax.numpy as jnp
from jax import lax
from jax.experimental import pallas as pl
from jax.experimental.pallas import tpu as pltpu
from jax.sharding import Mesh
from jax.sharding import PartitionSpec as P

Z, X, K, Y = "rows_z", "rows_x", "rows_k", "cls"
ROWS = (Z, X, K)
LANES = 128
INTERPRET = False

spread = 4.0
step_rate = 0.5

HIGHEST = lax.Precision.HIGHEST
LAST = (((1,), (1,)), ((), ()))
FIRST = (((0,), (0,)), ((), ()))


def gathered(value, axis):
    copies = jnp.broadcast_to(value, (lax.axis_size(axis), *value.shape))
    return lax.all_to_all(copies, axis, 0, 0, tiled=True)


def scattered(tiles, axis):
    return jnp.sum(lax.all_to_all(tiles, axis, 0, 0, tiled=True), axis=0)


def in_two(value):
    high = value.astype(jnp.bfloat16)
    low = (value - high.astype(jnp.float32)).astype(jnp.bfloat16)
    return high, low


def product(left, right, dims):
    (a, b), (c, d) = left, right
    one = lambda u, v: lax.dot_general(u, v, dims, preferred_element_type=jnp.float32)
    return one(a, d) + one(b, c) + one(a, c)


def kernel_products(
    place, own, other, first, second, third, fourth, coefficients, basis, sums, stacked
):
    chips, groups, depth, rows, width = own.shape
    blocks, lines, lanes = sums.shape
    classes, count = coefficients.shape
    split = basis.shape[2]
    padded = lines - blocks * split
    near = depth // blocks
    centers = (first, second, third, fourth)[:groups]
    is_low = place[2] == 0

    center_norm = jnp.zeros((1, count), jnp.float32)
    for piece in centers:
        wide = piece[...].astype(jnp.float32)
        center_norm += jnp.sum(wide * wide, axis=0, keepdims=True)
    stacked[padded - 8 : padded, :] = jnp.zeros((8, count), jnp.float32)
    stacked[:classes, :] = coefficients[...]
    stacked[padded:, :] = basis[:, pl.ds(place[0], 1)].reshape(-1, count)
    weights = in_two(stacked[...])

    for t in range(0, blocks, 2):
        inner = jnp.zeros((2 * lanes, count), jnp.float32)
        batch_norm = jnp.zeros((2 * lanes, 1), jnp.float32)
        for s in range(groups):
            y = lax.rem(place[0] + s, groups)
            pieces = []
            for z in range(t * near, (t + 2) * near):
                for x in range(chips):
                    a, b = own[x, y, z], other[x, y, z]
                    pieces += [jnp.where(is_low, a, b), jnp.where(is_low, b, a)]
            block = jnp.concatenate(pieces, axis=0)
            inner += jnp.dot(block, centers[s][...], preferred_element_type=jnp.float32)
            wide = block.astype(jnp.float32)
            batch_norm += jnp.sum(wide * wide, axis=1, keepdims=True)
        squared = center_norm + batch_norm - 2.0 * inner
        values = jnp.exp(-jnp.sqrt(jnp.maximum(squared, 0.0)) / spread)
        out = product(weights, in_two(values), LAST)
        for j in range(2):
            part = out[:, j * lanes : (j + 1) * lanes]
            sums[t + j, :padded, :] = part[:padded]
            at = padded + (t + j) * split
            sums[:, at : at + split, :] = part[padded:].reshape(blocks, split, lanes)


def gradient_of(place, predicted, labels, j, classes):
    cores, chips, rows, lanes = predicted.shape
    ids = lax.broadcasted_iota(jnp.int32, (rows, lanes), 0) + place[0] * classes
    return predicted[j // chips, j % chips] - (labels[j] == ids).astype(jnp.float32)


def project(place, predicted, first, second, third, fourth, labels, projected, *, classes):
    blocks, split, lanes = first.shape
    groups = projected.shape[1] // split
    pieces = (first, second, third, fourth)[:groups]
    total = jnp.zeros(projected.shape[1:], jnp.float32)
    for t in range(0, blocks, 2):
        pair = (t, t + 1)
        lines = [jnp.concatenate([p[j] for j in pair], axis=1) for p in pieces]
        gradient = [gradient_of(place, predicted, labels, j, classes) for j in pair]
        total += product(
            in_two(jnp.concatenate(lines, axis=0)),
            in_two(jnp.concatenate(gradient, axis=1)),
            LAST,
        )
    for s in range(groups):
        at = pl.multiple_of(lax.rem(place[0] + s, groups) * split, split)
        part = total[s * split : (s + 1) * split]
        projected[:, pl.ds(at, split), :] = jnp.broadcast_to(
            part[None], (projected.shape[0], *part.shape)
        )


def step_batch(place, predicted, labels, index, coefficients, output, updated):
    cores, chips, rows, lanes = predicted.shape
    classes, count = coefficients.shape
    total = jnp.zeros((rows, count), jnp.float32)
    slots = lax.broadcasted_iota(jnp.int32, (count, lanes), 0) + place[1] * count
    for t in range(0, cores * chips, 2):
        pair = (t, t + 1)
        gradient = [gradient_of(place, predicted, labels, j, classes) for j in pair]
        hits = [(index[j] == slots).astype(jnp.float32) for j in pair]
        spots = jnp.concatenate(hits, axis=1).astype(jnp.bfloat16)
        for part in in_two(jnp.concatenate(gradient, axis=1)):
            total += lax.dot_general(part, spots, LAST, preferred_element_type=jnp.float32)
        for j in pair:
            output[:, j * lanes : (j + 1) * lanes] = predicted[j // chips, j % chips, :classes]
    updated[...] = coefficients[...] - step_rate * total[:classes]


def correct(updated, projected, weights, result):
    classes = updated.shape[0]
    change = product(in_two(projected[...]), in_two(weights[...]), FIRST)
    result[...] = updated[...] + change[:classes]


def kernel(body, outs, name, scratch=(), **settings):
    near = pl.BlockSpec(memory_space=pltpu.VMEM)

    def call(*operands):
        return pl.pallas_call(
            functools.partial(body, **settings),
            out_shape=outs,
            in_specs=[
                pl.BlockSpec(memory_space=pltpu.SMEM) if o.size < 8 else near for o in operands
            ],
            out_specs=jax.tree.map(lambda _: near, outs),
            scratch_shapes=scratch,
            compiler_params=pltpu.CompilerParams(vmem_limit_bytes=24 * 2**20),
            interpret=INTERPRET,
            name=name,
        )(*operands)

    return call


def from_others(value, axis):
    size = lax.axis_size(axis)
    pieces = [value]
    for s in range(1, size):
        pieces.append(lax.ppermute(value, axis, [((d + s) % size, d) for d in range(size)]))
    return pieces + [value] * (4 - size)


def shards(
    centers,
    coefficients,
    batch_features,
    batch_labels,
    batch_index,
    subset_index,
    eigen_vectors,
    eigen_scale,
):
    depth, chips, cores, groups = (lax.axis_size(a) for a in (Z, X, K, Y))
    blocks = chips * cores
    count = centers.shape[0]
    classes = coefficients.shape[0]
    rank = lax.axis_index(ROWS)
    place = jnp.stack([lax.axis_index(Y), rank, lax.axis_index(K)]).astype(jnp.int32)
    vectors = eigen_vectors.shape[1]
    split = vectors // groups // blocks
    padded = -(-classes // 8) * 8
    while (padded + vectors // groups) % (8 * depth):
        padded += 8
    lines = padded + vectors // groups
    batch = blocks * LANES
    array = lambda *shape: jax.ShapeDtypeStruct(shape, jnp.float32)

    with jax.named_scope("centers_gather"):
        center_pieces = from_others(centers.T, Y)
    batch_own = batch_features
    for axis in (Z, Y, X):
        with jax.named_scope("batch_" + axis):
            batch_own = gathered(batch_own, axis)
        if axis == Z:
            batch_own, center_pieces = lax.optimization_barrier((batch_own, center_pieces))
    batch_other = from_others(batch_own, K)[1]

    spots = jnp.arange(count, dtype=jnp.int32) + rank * count
    chosen = (subset_index[:, None] == spots[None, :]).astype(jnp.float32)
    lifted = lax.dot_general(eigen_vectors, chosen, FIRST, precision=HIGHEST)
    weights = lifted * (step_rate * eigen_scale)[:, None]
    labels = batch_labels.reshape(blocks, 1, LANES)
    index = batch_index.reshape(blocks, 1, LANES)

    sums = kernel(
        kernel_products,
        array(blocks, lines, LANES),
        "kernel_products",
        (pltpu.VMEM((lines, count), jnp.float32),),
    )(
        place,
        batch_own,
        batch_other,
        *center_pieces,
        coefficients,
        lifted.reshape(blocks, groups, split, count),
    )

    own = scattered(sums.reshape(cores, chips, lines, LANES), K)
    own = scattered(own, X)
    own = scattered(own.reshape(depth, lines // depth, LANES), Z)
    own = gathered(own, Z).reshape(lines, LANES)
    with jax.named_scope("basis_gather"):
        basis = from_others(own[padded:].reshape(blocks, split, LANES), Y)
    predicted = gathered(gathered(own[:padded], X), K)

    copies = kernel(
        project, array(blocks, groups * split, padded), "project", classes=classes
    )(place, predicted, *basis, labels)
    with jax.named_scope("projected_gather"):
        projected = lax.all_to_all(
            copies, (X, K), 0, 0, tiled=True
        )
    projected = projected.reshape(chips, cores, -1, padded).swapaxes(0, 1)
    projected = projected.reshape(vectors, padded)

    output, updated = kernel(
        step_batch, (array(classes, batch), array(classes, count)), "step_batch"
    )(place, predicted, labels, index, coefficients)
    result = kernel(correct, array(classes, count), "correct")(updated, projected, weights)
    return (output, result)


def solution(mesh, shape=(16, 4, 2)):
    finer = Mesh(mesh.devices.reshape(*shape, mesh.shape["cls"]), (*ROWS, Y))
    placed = (P(ROWS, Y), P(Y, ROWS), P(ROWS, Y), P(), P(), P(ROWS), P(ROWS, None), P())
    return jax.shard_map(
        shards,
        mesh=finer,
        in_specs=placed,
        out_specs=(P(Y, None), P(Y, ROWS)),
        check_vma=False,
    )
```

```python
import functools

import jax
import jax.numpy as jnp
from jax import lax
from jax.experimental import pallas as pl
from jax.experimental.pallas import tpu as pltpu
from jax.sharding import Mesh
from jax.sharding import PartitionSpec as P

Z, X, K, Y = "rows_z", "rows_x", "rows_k", "cls"
ROWS = (Z, X, K)
LANES = 128
INTERPRET = False

spread = 4.0
step_rate = 0.5

HIGHEST = lax.Precision.HIGHEST
LAST = (((1,), (1,)), ((), ()))
FIRST = (((0,), (0,)), ((), ()))


def gathered(value, axis):
    copies = jnp.broadcast_to(value, (lax.axis_size(axis), *value.shape))
    return lax.all_to_all(copies, axis, 0, 0, tiled=True)


def scattered(tiles, axis):
    return jnp.sum(lax.all_to_all(tiles, axis, 0, 0, tiled=True), axis=0)


def in_two(value):
    high = value.astype(jnp.bfloat16)
    low = (value - high.astype(jnp.float32)).astype(jnp.bfloat16)
    return high, low


def product(left, right, dims):
    (a, b), (c, d) = left, right
    one = lambda u, v: lax.dot_general(u, v, dims, preferred_element_type=jnp.float32)
    return one(a, d) + one(b, c) + one(a, c)


def pack(batch, copies, granules):
    depth, rows, width = batch.shape
    full, rest = width // LANES, width % LANES
    half = depth // 2
    for z in range(depth):
        for h in range(full):
            granules[z * full + h] = batch[z, :, h * LANES : (h + 1) * LANES]
    for z in range(half):
        at = depth * full + z
        granules[at, :, :rest] = batch[z, :, full * LANES :]
        granules[at, :, rest:] = batch[z + half, :, full * LANES :]
    copies[...] = jnp.broadcast_to(granules[...][None], copies.shape)


def kernel_products(
    own, other, first, second, third, fourth, coefficients, basis, sums, stacked
):
    chips, groups, granules, rows, lanes = own.shape
    blocks, lines, _ = sums.shape
    classes, count = coefficients.shape
    full, rest = first.shape[0] // lanes, first.shape[0] % lanes
    depth = 2 * granules // (2 * full + 1)
    half = depth // 2
    split = basis.shape[2]
    padded = lines - blocks * split
    near = depth // blocks
    centers = (first, second, third, fourth)[:groups]
    is_low = lax.axis_index(K) == 0

    center_norm = jnp.zeros((1, count), jnp.float32)
    tails = []
    for piece in centers:
        wide = piece[...].astype(jnp.float32)
        center_norm += jnp.sum(wide * wide, axis=0, keepdims=True)
        tails.append(piece[full * lanes :])
    none = jnp.zeros((rest, count), tails[0].dtype)
    low_tail = jnp.concatenate([v for t in tails for v in (t, none)], axis=0)
    high_tail = jnp.concatenate([v for t in tails for v in (none, t)], axis=0)
    stacked[padded - 8 : padded, :] = jnp.zeros((8, count), jnp.float32)
    stacked[:classes, :] = coefficients[...]
    stacked[padded:, :] = basis[:, pl.ds(lax.axis_index(Y), 1)].reshape(-1, count)
    weights = in_two(stacked[...])
    lane = lax.broadcasted_iota(jnp.int32, (2 * lanes, lanes), 1)

    for t in range(0, blocks, 2):
        inner = jnp.zeros((2 * lanes, count), jnp.float32)
        batch_norm = jnp.zeros((2 * lanes, 1), jnp.float32)
        is_high = t * near >= half
        is_own = (lane >= rest) if is_high else (lane < rest)
        ends = []
        for s in range(groups):
            y = lax.rem(lax.axis_index(Y) + s, groups)
            columns = []
            for h in range(full + 1):
                pieces = []
                for z in range(t * near, (t + 2) * near):
                    at = z * full + h if h < full else depth * full + z % half
                    for x in range(chips):
                        a, b = own[x, y, at], other[x, y, at]
                        pieces += [jnp.where(is_low, a, b), jnp.where(is_low, b, a)]
                columns.append(jnp.concatenate(pieces, axis=0))
                wide = columns[h].astype(jnp.float32)
                wide = wide if h < full else jnp.where(is_own, wide, 0.0)
                batch_norm += jnp.sum(wide * wide, axis=1, keepdims=True)
            ends.append(columns.pop())
            inner += jnp.dot(
                jnp.concatenate(columns, axis=1),
                centers[s][: full * lanes],
                preferred_element_type=jnp.float32,
            )
        inner += jnp.dot(
            jnp.concatenate(ends, axis=1),
            high_tail if is_high else low_tail,
            preferred_element_type=jnp.float32,
        )
        squared = center_norm + batch_norm - 2.0 * inner
        values = jnp.exp(-jnp.sqrt(jnp.maximum(squared, 0.0)) / spread)
        out = product(weights, in_two(values), LAST)
        for j in range(2):
            part = out[:, j * lanes : (j + 1) * lanes]
            sums[t + j, :padded, :] = part[:padded]
            at = padded + (t + j) * split
            sums[:, at : at + split, :] = part[padded:].reshape(blocks, split, lanes)


def lift(vectors, scale, index, lifted, weights):
    count = weights.shape[1]
    slots = lax.broadcasted_iota(jnp.int32, (count, index.shape[1]), 0) + lax.axis_index(ROWS) * count
    hits = (index[...] == slots).astype(jnp.bfloat16)
    turned = vectors[...].T
    total = jnp.zeros(weights.shape, jnp.float32)
    for part in in_two(turned):
        total += lax.dot_general(part, hits, LAST, preferred_element_type=jnp.float32)
    lifted[...] = total.reshape(lifted.shape)
    column = jnp.broadcast_to(scale[...], (8, scale.shape[1])).T[:, :1]
    weights[...] = total * (step_rate * column)


def block_of(own, other, j):
    core, chip = j // own.shape[0], j % own.shape[0]
    return jnp.where(lax.axis_index(K) == core, own[chip], other[chip])


def gradient_of(own, other, labels, j, classes):
    rows, lanes = own.shape[1:]
    ids = lax.broadcasted_iota(jnp.int32, (rows, lanes), 0) + lax.axis_index(Y) * classes
    return block_of(own, other, j) - (labels[j] == ids).astype(jnp.float32)


def project(own, other, first, second, third, fourth, labels, projected, *, classes):
    blocks, split, lanes = first.shape
    groups = projected.shape[1] // split
    pieces = (first, second, third, fourth)[:groups]
    total = jnp.zeros(projected.shape[1:], jnp.float32)
    for t in range(0, blocks, 2):
        pair = (t, t + 1)
        lines = [jnp.concatenate([p[j] for j in pair], axis=1) for p in pieces]
        gradient = [gradient_of(own, other, labels, j, classes) for j in pair]
        total += product(
            in_two(jnp.concatenate(lines, axis=0)),
            in_two(jnp.concatenate(gradient, axis=1)),
            LAST,
        )
    for s in range(groups):
        at = pl.multiple_of(lax.rem(lax.axis_index(Y) + s, groups) * split, split)
        part = total[s * split : (s + 1) * split]
        projected[:, pl.ds(at, split), :] = jnp.broadcast_to(
            part[None], (projected.shape[0], *part.shape)
        )


def step_batch(own, other, labels, index, coefficients, output, updated):
    chips, rows, lanes = own.shape
    classes, count = coefficients.shape
    total = jnp.zeros((rows, count), jnp.float32)
    slots = lax.broadcasted_iota(jnp.int32, (count, lanes), 0) + lax.axis_index(ROWS) * count
    for t in range(0, 2 * chips, 2):
        pair = (t, t + 1)
        gradient = [gradient_of(own, other, labels, j, classes) for j in pair]
        hits = [(index[j] == slots).astype(jnp.float32) for j in pair]
        spots = jnp.concatenate(hits, axis=1).astype(jnp.bfloat16)
        for part in in_two(jnp.concatenate(gradient, axis=1)):
            total += lax.dot_general(part, spots, LAST, preferred_element_type=jnp.float32)
        for j in pair:
            output[:, j * lanes : (j + 1) * lanes] = block_of(own, other, j)[:classes]
    updated[...] = coefficients[...] - step_rate * total[:classes]


def correct(updated, projected, weights, result):
    classes = updated.shape[0]
    change = product(in_two(projected[...]), in_two(weights[...]), FIRST)
    result[...] = updated[...] + change[:classes]


def kernel(body, outs, name, scratch=(), limit=16, **settings):
    near = pl.BlockSpec(memory_space=pltpu.VMEM)

    def call(*operands):
        return pl.pallas_call(
            functools.partial(body, **settings),
            out_shape=outs,
            in_specs=[near for _ in operands],
            out_specs=jax.tree.map(lambda _: near, outs),
            scratch_shapes=scratch,
            compiler_params=pltpu.CompilerParams(vmem_limit_bytes=limit * 2**20),
            interpret=INTERPRET,
            name=name,
        )(*operands)

    return call


def from_others(value, axis):
    size = lax.axis_size(axis)
    pieces = [value]
    for s in range(1, size):
        pieces.append(lax.ppermute(value, axis, [((d + s) % size, d) for d in range(size)]))
    return pieces + [value] * (4 - size)


def shards(
    centers,
    coefficients,
    batch_features,
    batch_labels,
    batch_index,
    subset_index,
    eigen_vectors,
    eigen_scale,
):
    depth, chips, cores, groups = (lax.axis_size(a) for a in (Z, X, K, Y))
    blocks = chips * cores
    count = centers.shape[0]
    classes = coefficients.shape[0]
    vectors = eigen_vectors.shape[1]
    split = vectors // groups // blocks
    padded = -(-classes // 8) * 8
    while (padded + vectors // groups) % (8 * depth):
        padded += 8
    lines = padded + vectors // groups
    batch = blocks * LANES
    array = lambda *shape: jax.ShapeDtypeStruct(shape, jnp.float32)

    with jax.named_scope("centers_gather"):
        center_pieces = from_others(centers.T, Y)
    with jax.named_scope("batch_z"):
        batch_own = gathered(batch_features, Z)
    batch_own, center_pieces = lax.optimization_barrier((batch_own, center_pieces))
    rows, width = batch_features.shape
    granules = (depth * (2 * width // LANES) // 2, rows, LANES)
    copies = kernel(
        pack,
        jax.ShapeDtypeStruct((chips * groups, *granules), batch_own.dtype),
        "pack",
        (pltpu.VMEM(granules, batch_own.dtype),),
        limit=2,
    )(batch_own)
    with jax.named_scope("batch_xy"):
        batch_own = lax.all_to_all(copies, (X, Y), 0, 0, tiled=True)
    batch_own = batch_own.reshape(chips, groups, *granules)
    batch_other = from_others(batch_own, K)[1]

    lifted, weights = kernel(
        lift, (array(blocks, groups, split, count), array(vectors, count)), "lift", limit=4
    )(eigen_vectors, eigen_scale[None], subset_index[None])
    labels = batch_labels.reshape(blocks, 1, LANES)
    index = batch_index.reshape(blocks, 1, LANES)

    sums = kernel(
        kernel_products,
        array(blocks, lines, LANES),
        "kernel_products",
        (pltpu.VMEM((lines, count), jnp.float32),),
    )(
        batch_own,
        batch_other,
        *center_pieces,
        coefficients,
        lifted,
    )

    own = scattered(sums.reshape(cores, chips, lines, LANES), K)
    own = scattered(own, X)
    own = scattered(own.reshape(depth, lines // depth, LANES), Z)
    own = gathered(own, Z).reshape(lines, LANES)
    with jax.named_scope("basis_gather"):
        basis = from_others(own[padded:].reshape(blocks, split, LANES), Y)
    predicted, basis = lax.optimization_barrier((gathered(own[:padded], X), basis))
    predicted = from_others(predicted, K)[:2]

    copies = kernel(
        project, array(blocks, groups * split, padded), "project", classes=classes
    )(*predicted, *basis, labels)
    with jax.named_scope("projected_gather"):
        projected = lax.all_to_all(copies, (K, X), 0, 0, tiled=True).reshape(vectors, padded)

    output, updated = kernel(
        step_batch, (array(classes, batch), array(classes, count)), "step_batch"
    )(*predicted, labels, index, coefficients)
    result = kernel(correct, array(classes, count), "correct")(updated, projected, weights)
    return (output, result)


def solution(mesh, shape=(16, 4, 2)):
    finer = Mesh(mesh.devices.reshape(*shape, mesh.shape["cls"]), (*ROWS, Y))
    placed = (P(ROWS, Y), P(Y, ROWS), P(ROWS, Y), P(), P(), P(ROWS), P(ROWS, None), P())
    return jax.shard_map(
        shards,
        mesh=finer,
        in_specs=placed,
        out_specs=(P(Y, None), P(Y, ROWS)),
        check_vma=False,
    )
```

```python
import functools

import jax
import jax.numpy as jnp
from jax import lax
from jax.experimental import pallas as pl
from jax.experimental.pallas import tpu as pltpu
from jax.sharding import Mesh
from jax.sharding import PartitionSpec as P

Z, X, K, Y = "rows_z", "rows_x", "rows_k", "cls"
ROWS = (Z, X, K)
LANES = 128
INTERPRET = False

spread = 4.0
step_rate = 0.5

HIGHEST = lax.Precision.HIGHEST
LAST = (((1,), (1,)), ((), ()))
FIRST = (((0,), (0,)), ((), ()))


def gathered(value, axis):
    copies = jnp.broadcast_to(value, (lax.axis_size(axis), *value.shape))
    return lax.all_to_all(copies, axis, 0, 0, tiled=True)


def scattered(tiles, axis):
    return jnp.sum(lax.all_to_all(tiles, axis, 0, 0, tiled=True), axis=0)


def in_two(value):
    high = value.astype(jnp.bfloat16)
    low = (value - high.astype(jnp.float32)).astype(jnp.bfloat16)
    return high, low


def product(left, right, dims):
    (a, b), (c, d) = left, right
    one = lambda u, v: lax.dot_general(u, v, dims, preferred_element_type=jnp.float32)
    return one(a, d) + one(b, c) + one(a, c)


def fan(value, copies):
    copies[...] = jnp.broadcast_to(value[...][None], copies.shape)


def part(sums, copies, basis):
    padded = copies.shape[1]
    copies[...] = jnp.broadcast_to(sums[:padded][None], copies.shape)
    basis[...] = sums[padded:].reshape(basis.shape)


def pack(batch, copies, granules):
    depth, rows, width = batch.shape
    full, rest = width // LANES, width % LANES
    half = depth // 2
    for z in range(depth):
        for h in range(full):
            granules[z * full + h] = batch[z, :, h * LANES : (h + 1) * LANES]
    for z in range(half):
        at = depth * full + z
        granules[at, :, :rest] = batch[z, :, full * LANES :]
        granules[at, :, rest:] = batch[z + half, :, full * LANES :]
    copies[...] = jnp.broadcast_to(granules[...][None], copies.shape)


def kernel_products(
    own, other, first, second, third, fourth, coefficients, basis, sums, stacked
):
    chips, groups, granules, rows, lanes = own.shape
    blocks, lines, _ = sums.shape
    classes, count = coefficients.shape
    full, rest = first.shape[0] // lanes, first.shape[0] % lanes
    depth = 2 * granules // (2 * full + 1)
    half = depth // 2
    split = basis.shape[2]
    padded = lines - blocks * split
    near = depth // blocks
    centers = (first, second, third, fourth)[:groups]
    is_low = lax.axis_index(K) == 0

    center_norm = jnp.zeros((1, count), jnp.float32)
    tails = []
    for piece in centers:
        wide = piece[...].astype(jnp.float32)
        center_norm += jnp.sum(wide * wide, axis=0, keepdims=True)
        tails.append(piece[full * lanes :])
    none = jnp.zeros((rest, count), tails[0].dtype)
    low_tail = jnp.concatenate([v for t in tails for v in (t, none)], axis=0)
    high_tail = jnp.concatenate([v for t in tails for v in (none, t)], axis=0)
    stacked[padded - 8 : padded, :] = jnp.zeros((8, count), jnp.float32)
    stacked[:classes, :] = coefficients[...]
    stacked[padded:, :] = basis[:, pl.ds(lax.axis_index(Y), 1)].reshape(-1, count)
    weights = in_two(stacked[...])
    lane = lax.broadcasted_iota(jnp.int32, (2 * lanes, lanes), 1)

    for t in range(0, blocks, 2):
        inner = jnp.zeros((2 * lanes, count), jnp.float32)
        batch_norm = jnp.zeros((2 * lanes, 1), jnp.float32)
        is_high = t * near >= half
        is_own = (lane >= rest) if is_high else (lane < rest)
        ends = []
        for s in range(groups):
            y = lax.rem(lax.axis_index(Y) + s, groups)
            columns = []
            for h in range(full + 1):
                pieces = []
                for z in range(t * near, (t + 2) * near):
                    at = z * full + h if h < full else depth * full + z % half
                    for x in range(chips):
                        a, b = own[x, y, at], other[x, y, at]
                        pieces += [jnp.where(is_low, a, b), jnp.where(is_low, b, a)]
                columns.append(jnp.concatenate(pieces, axis=0))
                wide = columns[h].astype(jnp.float32)
                wide = wide if h < full else jnp.where(is_own, wide, 0.0)
                batch_norm += jnp.sum(wide * wide, axis=1, keepdims=True)
            ends.append(columns.pop())
            inner += jnp.dot(
                jnp.concatenate(columns, axis=1),
                centers[s][: full * lanes],
                preferred_element_type=jnp.float32,
            )
        inner += jnp.dot(
            jnp.concatenate(ends, axis=1),
            high_tail if is_high else low_tail,
            preferred_element_type=jnp.float32,
        )
        squared = center_norm + batch_norm - 2.0 * inner
        values = jnp.exp(-jnp.sqrt(jnp.maximum(squared, 0.0)) / spread)
        out = product(weights, in_two(values), LAST)
        for j in range(2):
            part = out[:, j * lanes : (j + 1) * lanes]
            sums[t + j, :padded, :] = part[:padded]
            at = padded + (t + j) * split
            sums[:, at : at + split, :] = part[padded:].reshape(blocks, split, lanes)


def lift(vectors, scale, index, lifted, weights):
    count = weights.shape[1]
    slots = lax.broadcasted_iota(jnp.int32, (count, index.shape[1]), 0) + lax.axis_index(ROWS) * count
    hits = (index[...] == slots).astype(jnp.bfloat16)
    turned = vectors[...].T
    total = jnp.zeros(weights.shape, jnp.float32)
    for part in in_two(turned):
        total += lax.dot_general(part, hits, LAST, preferred_element_type=jnp.float32)
    lifted[...] = total.reshape(lifted.shape)
    column = jnp.broadcast_to(scale[...], (8, scale.shape[1])).T[:, :1]
    weights[...] = total * (step_rate * column)


def block_of(own, other, j):
    core, chip = j // own.shape[0], j % own.shape[0]
    return jnp.where(lax.axis_index(K) == core, own[chip], other[chip])


def gradient_of(own, other, labels, j, classes):
    rows, lanes = own.shape[1:]
    ids = lax.broadcasted_iota(jnp.int32, (rows, lanes), 0) + lax.axis_index(Y) * classes
    return block_of(own, other, j) - (labels[j] == ids).astype(jnp.float32)


def project(own, other, first, second, third, fourth, labels, projected, *, classes):
    blocks, split, lanes = first.shape
    groups = projected.shape[1] // split
    pieces = (first, second, third, fourth)[:groups]
    total = jnp.zeros(projected.shape[1:], jnp.float32)
    for t in range(0, blocks, 2):
        pair = (t, t + 1)
        lines = [jnp.concatenate([p[j] for j in pair], axis=1) for p in pieces]
        gradient = [gradient_of(own, other, labels, j, classes) for j in pair]
        total += product(
            in_two(jnp.concatenate(lines, axis=0)),
            in_two(jnp.concatenate(gradient, axis=1)),
            LAST,
        )
    for s in range(groups):
        at = pl.multiple_of(lax.rem(lax.axis_index(Y) + s, groups) * split, split)
        part = total[s * split : (s + 1) * split]
        projected[:, pl.ds(at, split), :] = jnp.broadcast_to(
            part[None], (projected.shape[0], *part.shape)
        )


def step_batch(own, other, labels, index, coefficients, output, updated):
    chips, rows, lanes = own.shape
    classes, count = coefficients.shape
    total = jnp.zeros((rows, count), jnp.float32)
    slots = lax.broadcasted_iota(jnp.int32, (count, lanes), 0) + lax.axis_index(ROWS) * count
    for t in range(0, 2 * chips, 2):
        pair = (t, t + 1)
        gradient = [gradient_of(own, other, labels, j, classes) for j in pair]
        hits = [(index[j] == slots).astype(jnp.float32) for j in pair]
        spots = jnp.concatenate(hits, axis=1).astype(jnp.bfloat16)
        for part in in_two(jnp.concatenate(gradient, axis=1)):
            total += lax.dot_general(part, spots, LAST, preferred_element_type=jnp.float32)
        for j in pair:
            output[:, j * lanes : (j + 1) * lanes] = block_of(own, other, j)[:classes]
    updated[...] = coefficients[...] - step_rate * total[:classes]


def correct(updated, projected, weights, result):
    classes = updated.shape[0]
    change = product(in_two(projected[...]), in_two(weights[...]), FIRST)
    result[...] = updated[...] + change[:classes]


def kernel(body, outs, name, scratch=(), limit=16, **settings):
    near = pl.BlockSpec(memory_space=pltpu.VMEM)

    def call(*operands):
        return pl.pallas_call(
            functools.partial(body, **settings),
            out_shape=outs,
            in_specs=[near for _ in operands],
            out_specs=jax.tree.map(lambda _: near, outs),
            scratch_shapes=scratch,
            compiler_params=pltpu.CompilerParams(vmem_limit_bytes=limit * 2**20),
            interpret=INTERPRET,
            name=name,
        )(*operands)

    return call


def from_others(value, axis):
    size = lax.axis_size(axis)
    pieces = [value]
    for s in range(1, size):
        pieces.append(lax.ppermute(value, axis, [((d + s) % size, d) for d in range(size)]))
    return pieces + [value] * (4 - size)


def shards(
    centers,
    coefficients,
    batch_features,
    batch_labels,
    batch_index,
    subset_index,
    eigen_vectors,
    eigen_scale,
):
    depth, chips, cores, groups = (lax.axis_size(a) for a in (Z, X, K, Y))
    blocks = chips * cores
    count = centers.shape[0]
    classes = coefficients.shape[0]
    vectors = eigen_vectors.shape[1]
    split = vectors // groups // blocks
    padded = -(-classes // 8) * 8
    while (padded + vectors // groups) % (8 * depth):
        padded += 8
    lines = padded + vectors // groups
    batch = blocks * LANES
    array = lambda *shape: jax.ShapeDtypeStruct(shape, jnp.float32)

    with jax.named_scope("batch_z"):
        batch_own = lax.all_to_all(
            kernel(
                fan,
                jax.ShapeDtypeStruct((depth, *batch_features.shape), batch_features.dtype),
                "fan",
                limit=2,
            )(batch_features),
            Z,
            0,
            0,
            tiled=True,
        )
    batch_own, turned = lax.optimization_barrier((batch_own, centers.T))
    with jax.named_scope("centers_gather"):
        center_pieces = from_others(turned, Y)
    rows, width = batch_features.shape
    granules = (depth * (2 * width // LANES) // 2, rows, LANES)
    copies = kernel(
        pack,
        jax.ShapeDtypeStruct((chips * groups, *granules), batch_own.dtype),
        "pack",
        (pltpu.VMEM(granules, batch_own.dtype),),
        limit=2,
    )(batch_own)
    with jax.named_scope("batch_xy"):
        batch_own = lax.all_to_all(copies, (X, Y), 0, 0, tiled=True)
    batch_own, center_pieces = lax.optimization_barrier((batch_own, center_pieces))
    batch_own = batch_own.reshape(chips, groups, *granules)
    batch_other = from_others(batch_own, K)[1]

    lifted, weights = kernel(
        lift, (array(blocks, groups, split, count), array(vectors, count)), "lift", limit=4
    )(eigen_vectors, eigen_scale[None], subset_index[None])
    labels = batch_labels.reshape(blocks, 1, LANES)
    index = batch_index.reshape(blocks, 1, LANES)

    sums = kernel(
        kernel_products,
        array(blocks, lines, LANES),
        "kernel_products",
        (pltpu.VMEM((lines, count), jnp.float32),),
    )(
        batch_own,
        batch_other,
        *center_pieces,
        coefficients,
        lifted,
    )

    own = scattered(sums.reshape(cores, chips, lines, LANES), K)
    own = scattered(own, X)
    own = scattered(own.reshape(depth, lines // depth, LANES), Z)
    own = gathered(own, Z).reshape(lines, LANES)
    copies, basis = kernel(
        part, (array(chips, padded, LANES), array(blocks, split, LANES)), "part", limit=4
    )(own)
    with jax.named_scope("basis_gather"):
        basis = from_others(basis, Y)
    predicted = lax.all_to_all(copies, X, 0, 0, tiled=True)
    predicted, basis = lax.optimization_barrier((predicted, basis))
    predicted = from_others(predicted, K)[:2]

    copies = kernel(
        project, array(blocks, groups * split, padded), "project", classes=classes
    )(*predicted, *basis, labels)
    with jax.named_scope("projected_gather"):
        projected = lax.all_to_all(copies, (K, X), 0, 0, tiled=True).reshape(vectors, padded)

    output, updated = kernel(
        step_batch, (array(classes, batch), array(classes, count)), "step_batch"
    )(*predicted, labels, index, coefficients)
    result = kernel(correct, array(classes, count), "correct")(updated, projected, weights)
    return (output, result)


def solution(mesh, shape=(16, 4, 2)):
    finer = Mesh(mesh.devices.reshape(*shape, mesh.shape["cls"]), (*ROWS, Y))
    placed = (P(ROWS, Y), P(Y, ROWS), P(ROWS, Y), P(), P(), P(ROWS), P(ROWS, None), P())
    return jax.shard_map(
        shards,
        mesh=finer,
        in_specs=placed,
        out_specs=(P(Y, None), P(Y, ROWS)),
        check_vma=False,
    )
```

```python
import functools

import jax
import jax.numpy as jnp
from jax import lax
from jax.experimental import pallas as pl
from jax.experimental.pallas import tpu as pltpu
from jax.sharding import Mesh
from jax.sharding import PartitionSpec as P

Z, X, K, Y = "rows_z", "rows_x", "rows_k", "cls"
ROWS = (Z, X, K)
LANES = 128
INTERPRET = False

spread = 4.0
step_rate = 0.5

HIGHEST = lax.Precision.HIGHEST
LAST = (((1,), (1,)), ((), ()))
FIRST = (((0,), (0,)), ((), ()))


def gathered(value, axis):
    copies = jnp.broadcast_to(value, (lax.axis_size(axis), *value.shape))
    return lax.all_to_all(copies, axis, 0, 0, tiled=True)


def scattered(tiles, axis):
    return jnp.sum(lax.all_to_all(tiles, axis, 0, 0, tiled=True), axis=0)


def in_two(value):
    high = value.astype(jnp.bfloat16)
    low = (value - high.astype(jnp.float32)).astype(jnp.bfloat16)
    return high, low


def product(left, right, dims):
    (a, b), (c, d) = left, right
    one = lambda u, v: lax.dot_general(u, v, dims, preferred_element_type=jnp.float32)
    return one(a, d) + one(b, c) + one(a, c)


def fan(value, copies):
    copies[...] = jnp.broadcast_to(value[...][None], copies.shape)


def part(sums, copies, basis):
    padded = copies.shape[1]
    copies[...] = jnp.broadcast_to(sums[:padded][None], copies.shape)
    basis[...] = sums[padded:].reshape(basis.shape)


def pack(batch, copies, granules):
    depth, rows, width = batch.shape
    full, rest = width // LANES, width % LANES
    half = depth // 2
    for z in range(depth):
        for h in range(full):
            granules[z * full + h] = batch[z, :, h * LANES : (h + 1) * LANES]
    for z in range(half):
        at = depth * full + z
        granules[at, :, :rest] = batch[z, :, full * LANES :]
        granules[at, :, rest:] = batch[z + half, :, full * LANES :]
    copies[...] = jnp.broadcast_to(granules[...][None], copies.shape)


def kernel_products(
    own, other, first, second, third, fourth, coefficients, basis, sums, stacked
):
    chips, groups, granules, rows, lanes = own.shape
    blocks, lines, _ = sums.shape
    classes, count = coefficients.shape
    full, rest = first.shape[0] // lanes, first.shape[0] % lanes
    depth = 2 * granules // (2 * full + 1)
    half = depth // 2
    split = basis.shape[2]
    padded = lines - blocks * split
    near = depth // blocks
    centers = (first, second, third, fourth)[:groups]
    is_low = lax.axis_index(K) == 0

    center_norm = jnp.zeros((1, count), jnp.float32)
    tails = []
    for piece in centers:
        wide = piece[...].astype(jnp.float32)
        center_norm += jnp.sum(wide * wide, axis=0, keepdims=True)
        tails.append(piece[full * lanes :])
    none = jnp.zeros((rest, count), tails[0].dtype)
    low_tail = jnp.concatenate([v for t in tails for v in (t, none)], axis=0)
    high_tail = jnp.concatenate([v for t in tails for v in (none, t)], axis=0)
    stacked[padded - 8 : padded, :] = jnp.zeros((8, count), jnp.float32)
    stacked[:classes, :] = coefficients[...]
    stacked[padded:, :] = basis[:, pl.ds(lax.axis_index(Y), 1)].reshape(-1, count)
    weights = in_two(stacked[...])
    lane = lax.broadcasted_iota(jnp.int32, (2 * lanes, lanes), 1)

    for t in range(0, blocks, 2):
        inner = jnp.zeros((2 * lanes, count), jnp.float32)
        batch_norm = jnp.zeros((2 * lanes, 1), jnp.float32)
        is_high = t * near >= half
        is_own = (lane >= rest) if is_high else (lane < rest)
        ends = []
        for s in range(groups):
            y = lax.rem(lax.axis_index(Y) + s, groups)
            columns = []
            for h in range(full + 1):
                pieces = []
                for z in range(t * near, (t + 2) * near):
                    at = z * full + h if h < full else depth * full + z % half
                    for x in range(chips):
                        a, b = own[x, y, at], other[x, y, at]
                        pieces += [jnp.where(is_low, a, b), jnp.where(is_low, b, a)]
                columns.append(jnp.concatenate(pieces, axis=0))
                wide = columns[h].astype(jnp.float32)
                wide = wide if h < full else jnp.where(is_own, wide, 0.0)
                batch_norm += jnp.sum(wide * wide, axis=1, keepdims=True)
            ends.append(columns.pop())
            inner += jnp.dot(
                jnp.concatenate(columns, axis=1),
                centers[s][: full * lanes],
                preferred_element_type=jnp.float32,
            )
        inner += jnp.dot(
            jnp.concatenate(ends, axis=1),
            high_tail if is_high else low_tail,
            preferred_element_type=jnp.float32,
        )
        squared = center_norm + batch_norm - 2.0 * inner
        values = jnp.exp(-jnp.sqrt(jnp.maximum(squared, 0.0)) / spread)
        out = product(weights, in_two(values), LAST)
        for j in range(2):
            part = out[:, j * lanes : (j + 1) * lanes]
            sums[t + j, :padded, :] = part[:padded]
            at = padded + (t + j) * split
            sums[:, at : at + split, :] = part[padded:].reshape(blocks, split, lanes)


def lift(vectors, scale, index, lifted, weights):
    count = weights.shape[1]
    slots = lax.broadcasted_iota(jnp.int32, (count, index.shape[1]), 0) + lax.axis_index(ROWS) * count
    hits = (index[...] == slots).astype(jnp.bfloat16)
    turned = vectors[...].T
    total = jnp.zeros(weights.shape, jnp.float32)
    for part in in_two(turned):
        total += lax.dot_general(part, hits, LAST, preferred_element_type=jnp.float32)
    lifted[...] = total.reshape(lifted.shape)
    column = jnp.broadcast_to(scale[...], (8, scale.shape[1])).T[:, :1]
    weights[...] = total * (step_rate * column)


def block_of(own, other, j):
    core, chip = j // own.shape[0], j % own.shape[0]
    return jnp.where(lax.axis_index(K) == core, own[chip], other[chip])


def gradient_of(own, other, labels, j, classes):
    rows, lanes = own.shape[1:]
    ids = lax.broadcasted_iota(jnp.int32, (rows, lanes), 0) + lax.axis_index(Y) * classes
    return block_of(own, other, j) - (labels[j] == ids).astype(jnp.float32)


def project(own, other, first, second, third, fourth, labels, projected, *, classes):
    blocks, split, lanes = first.shape
    groups = projected.shape[1] // split
    pieces = (first, second, third, fourth)[:groups]
    total = jnp.zeros(projected.shape[1:], jnp.float32)
    for t in range(0, blocks, 2):
        pair = (t, t + 1)
        lines = [jnp.concatenate([p[j] for j in pair], axis=1) for p in pieces]
        gradient = [gradient_of(own, other, labels, j, classes) for j in pair]
        total += product(
            in_two(jnp.concatenate(lines, axis=0)),
            in_two(jnp.concatenate(gradient, axis=1)),
            LAST,
        )
    for s in range(groups):
        at = pl.multiple_of(lax.rem(lax.axis_index(Y) + s, groups) * split, split)
        part = total[s * split : (s + 1) * split]
        projected[:, pl.ds(at, split), :] = jnp.broadcast_to(
            part[None], (projected.shape[0], *part.shape)
        )


def step_batch(own, other, labels, index, coefficients, output, updated):
    chips, rows, lanes = own.shape
    classes, count = coefficients.shape
    total = jnp.zeros((rows, count), jnp.float32)
    slots = lax.broadcasted_iota(jnp.int32, (count, lanes), 0) + lax.axis_index(ROWS) * count
    for t in range(0, 2 * chips, 2):
        pair = (t, t + 1)
        gradient = [gradient_of(own, other, labels, j, classes) for j in pair]
        hits = [(index[j] == slots).astype(jnp.float32) for j in pair]
        spots = jnp.concatenate(hits, axis=1).astype(jnp.bfloat16)
        for part in in_two(jnp.concatenate(gradient, axis=1)):
            total += lax.dot_general(part, spots, LAST, preferred_element_type=jnp.float32)
        for j in pair:
            output[:, j * lanes : (j + 1) * lanes] = block_of(own, other, j)[:classes]
    updated[...] = coefficients[...] - step_rate * total[:classes]


def correct(updated, own, other, weights, result):
    classes, count = updated.shape
    lines = [block_of(own, other, j) for j in range(2 * own.shape[0])]
    projected = jnp.concatenate(lines, axis=0)
    change = product(in_two(projected), in_two(weights[...]), FIRST)
    result[...] = updated[...] + change[:classes]


def kernel(body, outs, name, scratch=(), limit=16, **settings):
    near = pl.BlockSpec(memory_space=pltpu.VMEM)

    def call(*operands):
        return pl.pallas_call(
            functools.partial(body, **settings),
            out_shape=outs,
            in_specs=[near for _ in operands],
            out_specs=jax.tree.map(lambda _: near, outs),
            scratch_shapes=scratch,
            compiler_params=pltpu.CompilerParams(vmem_limit_bytes=limit * 2**20),
            interpret=INTERPRET,
            name=name,
        )(*operands)

    return call


def from_next(value, axis):
    size = lax.axis_size(axis)
    return lax.ppermute(value, axis, [((d + 1) % size, d) for d in range(size)])


def from_others(value, axis):
    size = lax.axis_size(axis)
    pieces = [value]
    for s in range(1, size):
        pieces.append(lax.ppermute(value, axis, [((d + s) % size, d) for d in range(size)]))
    return pieces + [value] * (4 - size)


def shards(
    centers,
    coefficients,
    batch_features,
    batch_labels,
    batch_index,
    subset_index,
    eigen_vectors,
    eigen_scale,
):
    depth, chips, cores, groups = (lax.axis_size(a) for a in (Z, X, K, Y))
    blocks = chips * cores
    count = centers.shape[0]
    classes = coefficients.shape[0]
    vectors = eigen_vectors.shape[1]
    split = vectors // groups // blocks
    padded = -(-classes // 8) * 8
    while (padded + vectors // groups) % (8 * depth):
        padded += 8
    lines = padded + vectors // groups
    batch = blocks * LANES
    array = lambda *shape: jax.ShapeDtypeStruct(shape, jnp.float32)

    with jax.named_scope("batch_z"):
        batch_own = lax.all_to_all(
            kernel(
                fan,
                jax.ShapeDtypeStruct((depth, *batch_features.shape), batch_features.dtype),
                "fan",
                limit=2,
            )(batch_features),
            Z,
            0,
            0,
            tiled=True,
        )
    with jax.named_scope("centers_gather"):
        center_pieces = [centers.T, from_next(centers.T, Y)]
    batch_own, center_pieces = lax.optimization_barrier((batch_own, center_pieces))
    with jax.named_scope("centers_gather"):
        for _ in range(groups - 2):
            center_pieces.append(from_next(center_pieces[-1], Y))
    center_pieces += center_pieces[:1] * (4 - groups)
    rows, width = batch_features.shape
    granules = (depth * (2 * width // LANES) // 2, rows, LANES)
    copies = kernel(
        pack,
        jax.ShapeDtypeStruct((chips * groups, *granules), batch_own.dtype),
        "pack",
        (pltpu.VMEM(granules, batch_own.dtype),),
        limit=2,
    )(batch_own)
    with jax.named_scope("batch_xy"):
        batch_own = lax.all_to_all(copies, (X, Y), 0, 0, tiled=True)
    batch_own, center_pieces = lax.optimization_barrier((batch_own, center_pieces))
    batch_own = batch_own.reshape(chips, groups, *granules)
    batch_other = from_others(batch_own, K)[1]

    lifted, weights = kernel(
        lift, (array(blocks, groups, split, count), array(vectors, count)), "lift", limit=4
    )(eigen_vectors, eigen_scale[None], subset_index[None])
    labels = batch_labels.reshape(blocks, 1, LANES)
    index = batch_index.reshape(blocks, 1, LANES)

    sums = kernel(
        kernel_products,
        array(blocks, lines, LANES),
        "kernel_products",
        (pltpu.VMEM((lines, count), jnp.float32),),
    )(
        batch_own,
        batch_other,
        *center_pieces,
        coefficients,
        lifted,
    )

    own = scattered(sums.reshape(cores, chips, lines, LANES), K)
    own = scattered(own, X)
    own = scattered(own.reshape(depth, lines // depth, LANES), Z)
    own = gathered(own, Z).reshape(lines, LANES)
    copies, basis = kernel(
        part, (array(chips, padded, LANES), array(blocks, split, LANES)), "part", limit=4
    )(own)
    with jax.named_scope("basis_gather"):
        basis = from_others(basis, Y)
    predicted = lax.all_to_all(copies, X, 0, 0, tiled=True)
    predicted, basis = lax.optimization_barrier((predicted, basis))
    predicted = from_others(predicted, K)[:2]

    copies = kernel(
        project, array(chips, groups * split, padded), "project", classes=classes
    )(*predicted, *basis, labels)
    with jax.named_scope("projected_gather"):
        projected = lax.all_to_all(copies, X, 0, 0, tiled=True)
        projected = from_others(projected, K)[:2]

    output, updated = kernel(
        step_batch, (array(classes, batch), array(classes, count)), "step_batch"
    )(*predicted, labels, index, coefficients)
    result = kernel(correct, array(classes, count), "correct")(updated, *projected, weights)
    return (output, result)


def solution(mesh, shape=(16, 4, 2)):
    finer = Mesh(mesh.devices.reshape(*shape, mesh.shape["cls"]), (*ROWS, Y))
    placed = (P(ROWS, Y), P(Y, ROWS), P(ROWS, Y), P(), P(), P(ROWS), P(ROWS, None), P())
    return jax.shard_map(
        shards,
        mesh=finer,
        in_specs=placed,
        out_specs=(P(Y, None), P(Y, ROWS)),
        check_vma=False,
    )
```

```python
import functools

import jax
import jax.numpy as jnp
from jax import lax
from jax.experimental import pallas as pl
from jax.experimental.pallas import tpu as pltpu
from jax.sharding import Mesh
from jax.sharding import PartitionSpec as P

Z, X, K, Y = "rows_z", "rows_x", "rows_k", "cls"
ROWS = (Z, X, K)
LANES = 128
INTERPRET = False

spread = 4.0
step_rate = 0.5

HIGHEST = lax.Precision.HIGHEST
LAST = (((1,), (1,)), ((), ()))
FIRST = (((0,), (0,)), ((), ()))


def gathered(value, axis):
    copies = jnp.broadcast_to(value, (lax.axis_size(axis), *value.shape))
    return lax.all_to_all(copies, axis, 0, 0, tiled=True)


def scattered(tiles, axis):
    return jnp.sum(lax.all_to_all(tiles, axis, 0, 0, tiled=True), axis=0)


def in_two(value):
    high = value.astype(jnp.bfloat16)
    low = (value - high.astype(jnp.float32)).astype(jnp.bfloat16)
    return high, low


def product(left, right, dims):
    (a, b), (c, d) = left, right
    one = lambda u, v: lax.dot_general(u, v, dims, preferred_element_type=jnp.float32)
    return one(a, d) + one(b, c) + one(a, c)


def fan(value, copies):
    copies[...] = jnp.broadcast_to(value[...][None], copies.shape)


def part(sums, copies, basis):
    padded = copies.shape[1]
    copies[...] = jnp.broadcast_to(sums[:padded][None], copies.shape)
    basis[...] = sums[padded:].reshape(basis.shape)


def pack(batch, copies, granules):
    depth, rows, width = batch.shape
    full, rest = width // LANES, width % LANES
    half = depth // 2
    for z in range(depth):
        for h in range(full):
            granules[z * full + h] = batch[z, :, h * LANES : (h + 1) * LANES]
    for z in range(half):
        at = depth * full + z
        granules[at, :, :rest] = batch[z, :, full * LANES :]
        granules[at, :, rest:] = batch[z + half, :, full * LANES :]
    copies[...] = jnp.broadcast_to(granules[...][None], copies.shape)


def kernel_products(batch, first, second, third, fourth, high, low, sums, *, padded):
    chips, groups, granules, rows, lanes = batch.shape
    blocks, lines, _ = sums.shape
    count = high.shape[1]
    full, rest = first.shape[0] // lanes, first.shape[0] % lanes
    depth = 2 * granules // (2 * full + 1)
    half = depth // 2
    near = depth // blocks
    split = (lines - padded) // blocks
    centers = (first, second, third, fourth)[:groups]

    center_norm = jnp.zeros((1, count), jnp.float32)
    tails = []
    for piece in centers:
        wide = piece[...].astype(jnp.float32)
        center_norm += jnp.sum(wide * wide, axis=0, keepdims=True)
        tails.append(piece[full * lanes :])
    none = jnp.zeros((rest, count), tails[0].dtype)
    low_tail = jnp.concatenate([v for t in tails for v in (t, none)], axis=0)
    high_tail = jnp.concatenate([v for t in tails for v in (none, t)], axis=0)
    lane = lax.broadcasted_iota(jnp.int32, (2 * lanes, lanes), 1)

    for t in range(0, blocks, 2):
        inner = jnp.zeros((2 * lanes, count), jnp.float32)
        batch_norm = jnp.zeros((2 * lanes, 1), jnp.float32)
        is_high = t * near >= half
        is_own = (lane >= rest) if is_high else (lane < rest)
        ends = []
        for s in range(groups):
            y = lax.rem(lax.axis_index(Y) + s, groups)
            columns = []
            for h in range(full + 1):
                pieces = []
                for z in range(t * near, (t + 2) * near):
                    at = z * full + h if h < full else depth * full + z % half
                    pieces += [batch[x, y, at] for x in range(chips)]
                columns.append(jnp.concatenate(pieces, axis=0))
                wide = columns[h].astype(jnp.float32)
                wide = wide if h < full else jnp.where(is_own, wide, 0.0)
                batch_norm += jnp.sum(wide * wide, axis=1, keepdims=True)
            ends.append(columns.pop())
            inner += jnp.dot(
                jnp.concatenate(columns, axis=1),
                centers[s][: full * lanes],
                preferred_element_type=jnp.float32,
            )
        inner += jnp.dot(
            jnp.concatenate(ends, axis=1),
            high_tail if is_high else low_tail,
            preferred_element_type=jnp.float32,
        )
        squared = center_norm + batch_norm - 2.0 * inner
        values = jnp.exp(-jnp.sqrt(jnp.maximum(squared, 0.0)) / spread)
        out = product((high[...], low[...]), in_two(values), LAST)
        for j in range(2):
            part = out[:, j * lanes : (j + 1) * lanes]
            sums[t + j, :padded, :] = part[:padded]
            at = padded + (t + j) * split
            sums[:, at : at + split, :] = part[padded:].reshape(blocks, split, lanes)


def lift(vectors, scale, index, coefficients, high, low, weights, stacked):
    classes, count = coefficients.shape
    lines, groups = stacked.shape[0], lax.axis_size(Y)
    own = weights.shape[0] // groups
    padded = lines - own
    split = own // lax.axis_size(X)
    slots = lax.broadcasted_iota(jnp.int32, (count, index.shape[1]), 0)
    hits = index[...] == slots + lax.axis_index(ROWS) * count
    hits = hits.astype(jnp.float32).astype(jnp.bfloat16)
    turned = vectors[...].T
    total = jnp.zeros(weights.shape, jnp.float32)
    for part in in_two(turned):
        total += lax.dot_general(part, hits, LAST, preferred_element_type=jnp.float32)
    column = jnp.broadcast_to(scale[...], (8, scale.shape[1])).T[:, :1]
    stacked[padded - 8 : padded, :] = jnp.zeros((8, count), jnp.float32)
    stacked[:classes, :] = coefficients[...]
    weights[...] = total
    for x in range(lax.axis_size(X)):
        at = pl.multiple_of((x * groups + lax.axis_index(Y)) * split, split)
        stacked[padded + x * split : padded + (x + 1) * split, :] = weights[pl.ds(at, split), :]
    high[...], low[...] = in_two(stacked[...])
    weights[...] = total * (step_rate * column)


def add(own, other, total):
    total[...] = own[...] + other[...]


def join(own, other, copies):
    copies[...] = jnp.broadcast_to((own[...] + other[...])[None], copies.shape)


def targets_of(labels, j, rows, classes):
    ids = lax.broadcasted_iota(jnp.int32, (rows, 2 * LANES), 0) + lax.axis_index(Y) * classes
    return (labels[j] == ids).astype(jnp.float32)


def project(own, first, second, third, fourth, labels, projected, *, classes, rows_each):
    blocks, split, lanes = first.shape
    rows = own.shape[1]
    groups = projected.shape[0] // split
    pieces = (first, second, third, fourth)[:groups]
    side = 1 - lax.axis_index(K)
    spot = lax.broadcasted_iota(jnp.int32, (lanes, 2 * lanes), 0)
    lane = lax.broadcasted_iota(jnp.int32, (lanes, 2 * lanes), 1)
    line = spot // rows_each * (2 * rows_each) + side * rows_each + spot % rows_each
    picks = (lane == line).astype(jnp.float32).astype(jnp.bfloat16)
    total = jnp.zeros(projected.shape, jnp.float32)
    for t in range(0, blocks, 2):
        lines = [jnp.concatenate([p[t], p[t + 1]], axis=1) for p in pieces]
        gradient = []
        for j in (t, t + 1):
            targets = targets_of(labels, j, rows, classes).astype(jnp.bfloat16)
            hits = lax.dot_general(targets, picks, LAST, preferred_element_type=jnp.float32)
            gradient.append(own[j] - hits)
        total += product(
            in_two(jnp.concatenate(lines, axis=0)),
            in_two(jnp.concatenate(gradient, axis=1)),
            LAST,
        )
    for s in range(groups):
        at = pl.multiple_of(lax.rem(lax.axis_index(Y) + s, groups) * split, split)
        projected[pl.ds(at, split), :] = total[s * split : (s + 1) * split]


def step_batch(own, other, labels, index, coefficients, output, updated, *, rows_each):
    blocks, rows, lanes = own.shape
    classes, count = coefficients.shape
    total = jnp.zeros((rows, count), jnp.float32)
    slots = lax.broadcasted_iota(jnp.int32, (count, 2 * lanes), 0)
    slots += lax.axis_index(ROWS) * count
    spot = lax.broadcasted_iota(jnp.int32, (2 * lanes, 2 * lanes), 0)
    lane = lax.broadcasted_iota(jnp.int32, (2 * lanes, 2 * lanes), 1)
    core = jnp.where(spot < lanes, 1 - lax.axis_index(K), lax.axis_index(K))
    place = spot % lanes
    line = place // rows_each * (2 * rows_each) + core * rows_each + place % rows_each
    picks = (lane == line).astype(jnp.float32).astype(jnp.bfloat16)
    for j in range(blocks):
        rest = jnp.concatenate([own[j], other[j]], axis=1)
        predicted = jnp.zeros((rows, 2 * lanes), jnp.float32)
        for _ in range(3):
            part = rest.astype(jnp.bfloat16)
            predicted += jnp.dot(part, picks, preferred_element_type=jnp.float32)
            rest = rest - part.astype(jnp.float32)
        output[:, 2 * j * lanes : 2 * (j + 1) * lanes] = predicted[:classes]
        hits = (index[j] == slots).astype(jnp.float32).astype(jnp.bfloat16)
        for part in in_two(predicted - targets_of(labels, j, rows, classes)):
            total += lax.dot_general(part, hits, LAST, preferred_element_type=jnp.float32)
    updated[...] = coefficients[...] - step_rate * total[:classes]


def correct(updated, projected, weights, result):
    classes = updated.shape[0]
    change = product(in_two(projected[...]), in_two(weights[...]), FIRST)
    result[...] = updated[...] + change[:classes]


def kernel(body, outs, name, scratch=(), limit=16, **settings):
    near = pl.BlockSpec(memory_space=pltpu.VMEM)

    def call(*operands):
        return pl.pallas_call(
            functools.partial(body, **settings),
            out_shape=outs,
            in_specs=[near for _ in operands],
            out_specs=jax.tree.map(lambda _: near, outs),
            scratch_shapes=scratch,
            compiler_params=pltpu.CompilerParams(vmem_limit_bytes=limit * 2**20),
            interpret=INTERPRET,
            name=name,
        )(*operands)

    return call


def from_others(value, axis):
    size = lax.axis_size(axis)
    pieces = [value]
    for s in range(1, size):
        pieces.append(lax.ppermute(value, axis, [((d + s) % size, d) for d in range(size)]))
    return pieces + [value] * (4 - size)


def shards(
    centers,
    coefficients,
    batch_features,
    batch_labels,
    batch_index,
    subset_index,
    eigen_vectors,
    eigen_scale,
):
    depth, chips, groups = (lax.axis_size(a) for a in (Z, X, Y))
    count = centers.shape[0]
    classes = coefficients.shape[0]
    vectors = eigen_vectors.shape[1]
    split = vectors // groups // chips
    padded = -(-classes // 8) * 8
    while (padded + vectors // groups) % (8 * depth):
        padded += 8
    lines = padded + vectors // groups
    batch = batch_labels.shape[0]
    array = lambda *shape: jax.ShapeDtypeStruct(shape, jnp.float32)

    with jax.named_scope("batch_z"):
        batch_own = lax.all_to_all(
            kernel(
                fan,
                jax.ShapeDtypeStruct((depth, *batch_features.shape), batch_features.dtype),
                "fan",
                limit=2,
            )(batch_features),
            Z,
            0,
            0,
            tiled=True,
        )
    batch_own, turned = lax.optimization_barrier((batch_own, centers.T))
    with jax.named_scope("centers_gather"):
        center_pieces = from_others(turned, Y)
    rows, width = batch_features.shape
    granules = (depth * (2 * width // LANES) // 2, rows, LANES)
    copies = kernel(
        pack,
        jax.ShapeDtypeStruct((chips * groups, *granules), batch_own.dtype),
        "pack",
        (pltpu.VMEM(granules, batch_own.dtype),),
        limit=2,
    )(batch_own)
    with jax.named_scope("batch_xy"):
        batch_own = lax.all_to_all(copies, (X, Y), 0, 0, tiled=True)
    batch_own, center_pieces = lax.optimization_barrier((batch_own, center_pieces))
    batch_own = batch_own.reshape(chips, groups, *granules)
    batch_other = from_others(batch_own, K)[1]

    high, low, weights = kernel(
        lift,
        (
            jax.ShapeDtypeStruct((lines, count), jnp.bfloat16),
            jax.ShapeDtypeStruct((lines, count), jnp.bfloat16),
            array(vectors, count),
        ),
        "lift",
        (pltpu.VMEM((lines, count), jnp.float32),),
        limit=6,
    )(eigen_vectors, eigen_scale[None], subset_index[None], coefficients)
    labels = batch_labels.reshape(chips, 1, 2 * LANES)
    index = batch_index.reshape(chips, 1, 2 * LANES)

    products = kernel(
        kernel_products, array(chips, lines, LANES), "kernel_products", limit=12, padded=padded
    )
    sent = from_others(products(batch_own, *center_pieces, high, low), K)[1]
    kept = products(batch_other, *center_pieces, high, low)
    own = kernel(add, array(chips, lines, LANES), "add", limit=6)(kept, sent)

    own = scattered(own, X)
    own = scattered(own.reshape(depth, lines // depth, LANES), Z)
    own = gathered(own, Z).reshape(lines, LANES)
    copies, basis = kernel(
        part, (array(chips, padded, LANES), array(chips, split, LANES)), "part", limit=4
    )(own)
    with jax.named_scope("basis_gather"):
        basis = from_others(basis, Y)
    predicted = lax.all_to_all(copies, X, 0, 0, tiled=True)
    predicted, basis = lax.optimization_barrier((predicted, basis))

    half = kernel(
        project, array(groups * split, padded), "project", classes=classes, rows_each=rows
    )(predicted, *basis, labels)
    copies = kernel(join, array(chips, groups * split, padded), "join", limit=4)(
        *from_others(half, K)[:2]
    )
    copies, late = lax.optimization_barrier((copies, predicted))
    with jax.named_scope("projected_gather"):
        projected = lax.all_to_all(copies, X, 0, 0, tiled=True).reshape(vectors, padded)

    output, updated = kernel(
        step_batch,
        (array(classes, batch), array(classes, count)),
        "step_batch",
        rows_each=rows,
    )(*from_others(late, K)[:2], labels, index, coefficients)
    result = kernel(correct, array(classes, count), "correct")(updated, projected, weights)
    return (output, result)


def solution(mesh, shape=(16, 4, 2)):
    finer = Mesh(mesh.devices.reshape(*shape, mesh.shape["cls"]), (*ROWS, Y))
    placed = (P(ROWS, Y), P(Y, ROWS), P(ROWS, Y), P(), P(), P(ROWS), P(ROWS, None), P())
    return jax.shard_map(
        shards,
        mesh=finer,
        in_specs=placed,
        out_specs=(P(Y, None), P(Y, ROWS)),
        check_vma=False,
    )
```

```python
import functools

import jax
import jax.numpy as jnp
from jax import lax
from jax.experimental import pallas as pl
from jax.experimental.pallas import tpu as pltpu
from jax.sharding import Mesh
from jax.sharding import PartitionSpec as P

Z, X, K, Y = "rows_z", "rows_x", "rows_k", "cls"
ROWS = (Z, X, K)
LANES = 128
INTERPRET = False

spread = 4.0
step_rate = 0.5

HIGHEST = lax.Precision.HIGHEST
LAST = (((1,), (1,)), ((), ()))
FIRST = (((0,), (0,)), ((), ()))


def gathered(value, axis):
    copies = jnp.broadcast_to(value, (lax.axis_size(axis), *value.shape))
    return lax.all_to_all(copies, axis, 0, 0, tiled=True)


def scattered(tiles, axis):
    return jnp.sum(lax.all_to_all(tiles, axis, 0, 0, tiled=True), axis=0)


def in_two(value):
    high = value.astype(jnp.bfloat16)
    low = (value - high.astype(jnp.float32)).astype(jnp.bfloat16)
    return high, low


def product(left, right, dims):
    (a, b), (c, d) = left, right
    one = lambda u, v: lax.dot_general(u, v, dims, preferred_element_type=jnp.float32)
    return one(a, d) + one(b, c) + one(a, c)


def fan(value, copies):
    copies[...] = jnp.broadcast_to(value[...][None], copies.shape)


def part(sums, copies, basis):
    padded = copies.shape[1]
    copies[...] = jnp.broadcast_to(sums[:padded][None], copies.shape)
    basis[...] = sums[padded:].reshape(basis.shape)


def pair(own, other, both):
    both[0] = own[...]
    both[1] = other[...]


def group_of(s):
    y, groups = lax.axis_index(Y), lax.axis_size(Y)
    y = y if s < 2 else groups - 1 - y
    return y + (1 - 2 * lax.rem(y, 2)) if s % 2 else y


def pack(batch, copies, granules):
    depth, rows, width = batch.shape
    full, rest = width // LANES, width % LANES
    half = depth // 2
    for z in range(depth):
        for h in range(full):
            granules[z * full + h] = batch[z, :, h * LANES : (h + 1) * LANES]
    for z in range(half):
        at = depth * full + z
        granules[at, :, :rest] = batch[z, :, full * LANES :]
        granules[at, :, rest:] = batch[z + half, :, full * LANES :]
    copies[...] = jnp.broadcast_to(granules[...][None], copies.shape)


def kernel_products(batch, near_pair, far_pair, high, low, sums, *, padded):
    chips, groups, granules, rows, lanes = batch.shape
    blocks, lines, _ = sums.shape
    count = high.shape[1]
    full, rest = near_pair.shape[1] // lanes, near_pair.shape[1] % lanes
    depth = 2 * granules // (2 * full + 1)
    half = depth // 2
    near = depth // blocks
    split = (lines - padded) // blocks
    centers = [p.at[i] for p in (near_pair, far_pair) for i in range(2)][:groups]

    center_norm = jnp.zeros((1, count), jnp.float32)
    tails = []
    for piece in centers:
        wide = piece[...].astype(jnp.float32)
        center_norm += jnp.sum(wide * wide, axis=0, keepdims=True)
        tails.append(piece[full * lanes :])
    none = jnp.zeros((rest, count), tails[0].dtype)
    low_tail = jnp.concatenate([v for t in tails for v in (t, none)], axis=0)
    high_tail = jnp.concatenate([v for t in tails for v in (none, t)], axis=0)
    lane = lax.broadcasted_iota(jnp.int32, (2 * lanes, lanes), 1)

    for t in range(0, blocks, 2):
        inner = jnp.zeros((2 * lanes, count), jnp.float32)
        batch_norm = jnp.zeros((2 * lanes, 1), jnp.float32)
        is_high = t * near >= half
        is_own = (lane >= rest) if is_high else (lane < rest)
        ends = []
        for s in range(groups):
            y = group_of(s)
            columns = []
            for h in range(full + 1):
                pieces = []
                for z in range(t * near, (t + 2) * near):
                    at = z * full + h if h < full else depth * full + z % half
                    pieces += [batch[x, y, at] for x in range(chips)]
                columns.append(jnp.concatenate(pieces, axis=0))
                wide = columns[h].astype(jnp.float32)
                wide = wide if h < full else jnp.where(is_own, wide, 0.0)
                batch_norm += jnp.sum(wide * wide, axis=1, keepdims=True)
            ends.append(columns.pop())
            inner += jnp.dot(
                jnp.concatenate(columns, axis=1),
                centers[s][: full * lanes],
                preferred_element_type=jnp.float32,
            )
        inner += jnp.dot(
            jnp.concatenate(ends, axis=1),
            high_tail if is_high else low_tail,
            preferred_element_type=jnp.float32,
        )
        squared = center_norm + batch_norm - 2.0 * inner
        values = jnp.exp(-jnp.sqrt(jnp.maximum(squared, 0.0)) / spread)
        out = product((high[...], low[...]), in_two(values), LAST)
        for j in range(2):
            part = out[:, j * lanes : (j + 1) * lanes]
            sums[t + j, :padded, :] = part[:padded]
            at = padded + (t + j) * split
            sums[:, at : at + split, :] = part[padded:].reshape(blocks, split, lanes)


def lift(vectors, scale, index, coefficients, high, low, weights, stacked):
    classes, count = coefficients.shape
    lines, groups = stacked.shape[0], lax.axis_size(Y)
    own = weights.shape[0] // groups
    padded = lines - own
    split = own // lax.axis_size(X)
    slots = lax.broadcasted_iota(jnp.int32, (count, index.shape[1]), 0)
    hits = index[...] == slots + lax.axis_index(ROWS) * count
    hits = hits.astype(jnp.float32).astype(jnp.bfloat16)
    turned = vectors[...].T
    total = jnp.zeros(weights.shape, jnp.float32)
    for part in in_two(turned):
        total += lax.dot_general(part, hits, LAST, preferred_element_type=jnp.float32)
    column = jnp.broadcast_to(scale[...], (8, scale.shape[1])).T[:, :1]
    stacked[padded - 8 : padded, :] = jnp.zeros((8, count), jnp.float32)
    stacked[:classes, :] = coefficients[...]
    weights[...] = total
    for x in range(lax.axis_size(X)):
        at = pl.multiple_of((x * groups + lax.axis_index(Y)) * split, split)
        stacked[padded + x * split : padded + (x + 1) * split, :] = weights[pl.ds(at, split), :]
    high[...], low[...] = in_two(stacked[...])
    weights[...] = total * (step_rate * column)


def add(own, other, total):
    total[...] = own[...] + other[...]


def join(own, other, copies):
    copies[...] = jnp.broadcast_to((own[...] + other[...])[None], copies.shape)


def targets_of(labels, j, rows, classes):
    ids = lax.broadcasted_iota(jnp.int32, (rows, 2 * LANES), 0) + lax.axis_index(Y) * classes
    return (labels[j] == ids).astype(jnp.float32)


def project(own, near_pair, far_pair, labels, projected, *, classes, rows_each):
    _, blocks, split, lanes = near_pair.shape
    rows = own.shape[1]
    groups = projected.shape[0] // split
    pieces = [p.at[i] for p in (near_pair, far_pair) for i in range(2)][:groups]
    side = 1 - lax.axis_index(K)
    spot = lax.broadcasted_iota(jnp.int32, (lanes, 2 * lanes), 0)
    lane = lax.broadcasted_iota(jnp.int32, (lanes, 2 * lanes), 1)
    line = spot // rows_each * (2 * rows_each) + side * rows_each + spot % rows_each
    picks = (lane == line).astype(jnp.float32).astype(jnp.bfloat16)
    total = jnp.zeros(projected.shape, jnp.float32)
    for t in range(0, blocks, 2):
        lines = [jnp.concatenate([p[t], p[t + 1]], axis=1) for p in pieces]
        gradient = []
        for j in (t, t + 1):
            targets = targets_of(labels, j, rows, classes).astype(jnp.bfloat16)
            hits = lax.dot_general(targets, picks, LAST, preferred_element_type=jnp.float32)
            gradient.append(own[j] - hits)
        total += product(
            in_two(jnp.concatenate(lines, axis=0)),
            in_two(jnp.concatenate(gradient, axis=1)),
            LAST,
        )
    for s in range(groups):
        at = pl.multiple_of(group_of(s) * split, split)
        projected[pl.ds(at, split), :] = total[s * split : (s + 1) * split]


def step_batch(own, other, labels, index, coefficients, output, updated, *, rows_each):
    blocks, rows, lanes = own.shape
    classes, count = coefficients.shape
    total = jnp.zeros((rows, count), jnp.float32)
    slots = lax.broadcasted_iota(jnp.int32, (count, 2 * lanes), 0)
    slots += lax.axis_index(ROWS) * count
    spot = lax.broadcasted_iota(jnp.int32, (2 * lanes, 2 * lanes), 0)
    lane = lax.broadcasted_iota(jnp.int32, (2 * lanes, 2 * lanes), 1)
    core = jnp.where(spot < lanes, 1 - lax.axis_index(K), lax.axis_index(K))
    place = spot % lanes
    line = place // rows_each * (2 * rows_each) + core * rows_each + place % rows_each
    picks = (lane == line).astype(jnp.float32).astype(jnp.bfloat16)
    for j in range(blocks):
        rest = jnp.concatenate([own[j], other[j]], axis=1)
        predicted = jnp.zeros((rows, 2 * lanes), jnp.float32)
        for _ in range(3):
            part = rest.astype(jnp.bfloat16)
            predicted += jnp.dot(part, picks, preferred_element_type=jnp.float32)
            rest = rest - part.astype(jnp.float32)
        output[:, 2 * j * lanes : 2 * (j + 1) * lanes] = predicted[:classes]
        hits = (index[j] == slots).astype(jnp.float32).astype(jnp.bfloat16)
        for part in in_two(predicted - targets_of(labels, j, rows, classes)):
            total += lax.dot_general(part, hits, LAST, preferred_element_type=jnp.float32)
    updated[...] = coefficients[...] - step_rate * total[:classes]


def correct(updated, projected, weights, result):
    classes = updated.shape[0]
    change = product(in_two(projected[...]), in_two(weights[...]), FIRST)
    result[...] = updated[...] + change[:classes]


def kernel(body, outs, name, scratch=(), limit=16, **settings):
    near = pl.BlockSpec(memory_space=pltpu.VMEM)

    def call(*operands):
        return pl.pallas_call(
            functools.partial(body, **settings),
            out_shape=outs,
            in_specs=[near for _ in operands],
            out_specs=jax.tree.map(lambda _: near, outs),
            scratch_shapes=scratch,
            compiler_params=pltpu.CompilerParams(vmem_limit_bytes=limit * 2**20),
            interpret=INTERPRET,
            name=name,
        )(*operands)

    return call


def swapped(value, axis, mirrored=False):
    size = lax.axis_size(axis)
    other = (lambda d: size - 1 - d) if mirrored else (lambda d: d ^ 1)
    return lax.ppermute(value, axis, [(other(d), d) for d in range(size)])


def paired(own, other):
    out = jax.ShapeDtypeStruct((2, *own.shape), own.dtype)
    return kernel(pair, out, "pair", limit=2)(own, other)


def shards(
    centers,
    coefficients,
    batch_features,
    batch_labels,
    batch_index,
    subset_index,
    eigen_vectors,
    eigen_scale,
):
    depth, chips, groups = (lax.axis_size(a) for a in (Z, X, Y))
    count = centers.shape[0]
    classes = coefficients.shape[0]
    vectors = eigen_vectors.shape[1]
    split = vectors // groups // chips
    padded = -(-classes // 8) * 8
    while (padded + vectors // groups) % (8 * depth):
        padded += 8
    lines = padded + vectors // groups
    batch = batch_labels.shape[0]
    array = lambda *shape: jax.ShapeDtypeStruct(shape, jnp.float32)

    with jax.named_scope("batch_z"):
        batch_own = lax.all_to_all(
            kernel(
                fan,
                jax.ShapeDtypeStruct((depth, *batch_features.shape), batch_features.dtype),
                "fan",
                limit=2,
            )(batch_features),
            Z,
            0,
            0,
            tiled=True,
        )
    with jax.named_scope("centers_gather"):
        near_centers = paired(centers.T, swapped(centers.T, Y))
    batch_own, near_centers = lax.optimization_barrier((batch_own, near_centers))
    with jax.named_scope("centers_gather"):
        far_centers = swapped(near_centers, Y, True)
    rows, width = batch_features.shape
    granules = (depth * (2 * width // LANES) // 2, rows, LANES)
    copies = kernel(
        pack,
        jax.ShapeDtypeStruct((chips * groups, *granules), batch_own.dtype),
        "pack",
        (pltpu.VMEM(granules, batch_own.dtype),),
        limit=2,
    )(batch_own)
    with jax.named_scope("batch_xy"):
        batch_own = lax.all_to_all(copies, (X, Y), 0, 0, tiled=True)
    batch_own, far_centers = lax.optimization_barrier((batch_own, far_centers))
    batch_own = batch_own.reshape(chips, groups, *granules)
    batch_other = swapped(batch_own, K)

    high, low, weights = kernel(
        lift,
        (
            jax.ShapeDtypeStruct((lines, count), jnp.bfloat16),
            jax.ShapeDtypeStruct((lines, count), jnp.bfloat16),
            array(vectors, count),
        ),
        "lift",
        (pltpu.VMEM((lines, count), jnp.float32),),
        limit=6,
    )(eigen_vectors, eigen_scale[None], subset_index[None], coefficients)
    labels = batch_labels.reshape(chips, 1, 2 * LANES)
    index = batch_index.reshape(chips, 1, 2 * LANES)

    products = kernel(
        kernel_products, array(chips, lines, LANES), "kernel_products", limit=12, padded=padded
    )
    sent = swapped(products(batch_own, near_centers, far_centers, high, low), K)
    kept = products(batch_other, near_centers, far_centers, high, low)
    own = kernel(add, array(chips, lines, LANES), "add", limit=6)(kept, sent)

    own = scattered(own, X)
    own = scattered(own.reshape(depth, lines // depth, LANES), Z)
    own = gathered(own, Z).reshape(lines, LANES)
    copies, basis = kernel(
        part, (array(chips, padded, LANES), array(chips, split, LANES)), "part", limit=4
    )(own)
    with jax.named_scope("basis_gather"):
        basis = paired(basis, swapped(basis, Y))
        basis = (basis, swapped(basis, Y, True))
    predicted = lax.all_to_all(copies, X, 0, 0, tiled=True)
    predicted, basis = lax.optimization_barrier((predicted, basis))

    half = kernel(
        project, array(groups * split, padded), "project", classes=classes, rows_each=rows
    )(predicted, *basis, labels)
    copies = kernel(join, array(chips, groups * split, padded), "join", limit=4)(
        half, swapped(half, K)
    )
    copies, late = lax.optimization_barrier((copies, predicted))
    with jax.named_scope("projected_gather"):
        projected = lax.all_to_all(copies, X, 0, 0, tiled=True).reshape(vectors, padded)

    output, updated = kernel(
        step_batch,
        (array(classes, batch), array(classes, count)),
        "step_batch",
        rows_each=rows,
    )(late, swapped(late, K), labels, index, coefficients)
    result = kernel(correct, array(classes, count), "correct")(updated, projected, weights)
    return (output, result)


def solution(mesh, shape=(16, 4, 2)):
    finer = Mesh(mesh.devices.reshape(*shape, mesh.shape["cls"]), (*ROWS, Y))
    placed = (P(ROWS, Y), P(Y, ROWS), P(ROWS, Y), P(), P(), P(ROWS), P(ROWS, None), P())
    return jax.shard_map(
        shards,
        mesh=finer,
        in_specs=placed,
        out_specs=(P(Y, None), P(Y, ROWS)),
        check_vma=False,
    )
```

```python
import functools

import jax
import jax.numpy as jnp
from jax import lax
from jax.experimental import pallas as pl
from jax.experimental.pallas import tpu as pltpu
from jax.sharding import Mesh
from jax.sharding import PartitionSpec as P


Z, X, K, Y = "rows_z", "rows_x", "rows_k", "cls"
ROWS = (Z, X, K)
LANES = 128
INTERPRET = False

CODES = 32767.0

spread = 4.0
step_rate = 0.5

LAST = (((1,), (1,)), ((), ()))
FIRST = (((0,), (0,)), ((), ()))


def gathered(value, axis):
    copies = jnp.broadcast_to(value, (lax.axis_size(axis), *value.shape))
    return lax.all_to_all(copies, axis, 0, 0, tiled=True)


def scattered(tiles, axis):
    return jnp.sum(lax.all_to_all(tiles, axis, 0, 0, tiled=True), axis=0)


def in_two(value):
    high = value.astype(jnp.bfloat16)
    low = (value - high.astype(jnp.float32)).astype(jnp.bfloat16)
    return high, low


def product(left, right, dims):
    (a, b), (c, d) = left, right
    one = lambda u, v: lax.dot_general(u, v, dims, preferred_element_type=jnp.float32)
    return one(a, d) + one(b, c) + one(a, c)


def fan(value, copies):
    copies[...] = jnp.broadcast_to(value[...][None], copies.shape)


def part(sums, copies, basis):
    padded = copies.shape[1]
    copies[...] = jnp.broadcast_to(sums[:padded][None], copies.shape)
    basis[...] = sums[padded:].reshape(basis.shape)


def pack(batch, copies, granules):
    depth, _, width = batch.shape
    full, rest = width // LANES, width % LANES
    half = depth // 2
    for z in range(depth):
        for h in range(full):
            granules[z * full + h] = batch[z, :, h * LANES : (h + 1) * LANES]
    for z in range(half):
        at = depth * full + z
        granules[at, :, :rest] = batch[z, :, full * LANES :]
        granules[at, :, rest:] = batch[z + half, :, full * LANES :]
    copies[...] = jnp.broadcast_to(granules[...][None], copies.shape)


def kernel_products(batch, first, second, third, fourth, high, low, sums, *, padded):
    chips, groups, granules, _, lanes = batch.shape
    blocks, lines, _ = sums.shape
    count = high.shape[1]
    full, rest = first.shape[0] // lanes, first.shape[0] % lanes
    depth = 2 * granules // (2 * full + 1)
    half = depth // 2
    near = depth // blocks
    split = (lines - padded) // blocks
    centers = (first, second, third, fourth)[:groups]

    center_norm = jnp.zeros((1, count), jnp.float32)
    tails = []
    for piece in centers:
        wide = piece[...].astype(jnp.float32)
        center_norm += jnp.sum(wide * wide, axis=0, keepdims=True)
        tails.append(piece[full * lanes :])
    none = jnp.zeros((rest, count), tails[0].dtype)
    low_tail = jnp.concatenate([v for t in tails for v in (t, none)], axis=0)
    high_tail = jnp.concatenate([v for t in tails for v in (none, t)], axis=0)
    lane = lax.broadcasted_iota(jnp.int32, (2 * lanes, lanes), 1)

    for t in range(0, blocks, 2):
        inner = jnp.zeros((2 * lanes, count), jnp.float32)
        batch_norm = jnp.zeros((2 * lanes, 1), jnp.float32)
        is_high = t * near >= half
        is_own = (lane >= rest) if is_high else (lane < rest)
        ends = []
        for s in range(groups):
            y = lax.rem(lax.axis_index(Y) + s, groups)
            columns = []
            for h in range(full + 1):
                pieces = []
                for z in range(t * near, (t + 2) * near):
                    at = z * full + h if h < full else depth * full + z % half
                    pieces += [batch[x, y, at] for x in range(chips)]
                columns.append(jnp.concatenate(pieces, axis=0))
                wide = columns[h].astype(jnp.float32)
                wide = wide if h < full else jnp.where(is_own, wide, 0.0)
                batch_norm += jnp.sum(wide * wide, axis=1, keepdims=True)
            ends.append(columns.pop())
            inner += jnp.dot(
                jnp.concatenate(columns, axis=1),
                centers[s][: full * lanes],
                preferred_element_type=jnp.float32,
            )
        inner += jnp.dot(
            jnp.concatenate(ends, axis=1),
            high_tail if is_high else low_tail,
            preferred_element_type=jnp.float32,
        )
        squared = center_norm + batch_norm - 2.0 * inner
        values = jnp.exp(-jnp.sqrt(jnp.maximum(squared, 0.0)) / spread)
        out = product((high[...], low[...]), in_two(values), LAST)
        for j in range(2):
            part = out[:, j * lanes : (j + 1) * lanes]
            sums[t + j, :padded, :] = part[:padded]
            at = padded + (t + j) * split
            sums[:, at : at + split, :] = part[padded:].reshape(blocks, split, lanes)


def lift(vectors, scale, index, coefficients, high, low, weights, stacked):
    classes, count = coefficients.shape
    lines, groups = stacked.shape[0], lax.axis_size(Y)
    own = weights.shape[0] // groups
    padded = lines - own
    split = own // lax.axis_size(X)
    slots = lax.broadcasted_iota(jnp.int32, (count, index.shape[1]), 0)
    hits = index[...] == slots + lax.axis_index(ROWS) * count
    hits = hits.astype(jnp.float32).astype(jnp.bfloat16)
    turned = vectors[...].T
    total = jnp.zeros(weights.shape, jnp.float32)
    for part in in_two(turned):
        total += lax.dot_general(part, hits, LAST, preferred_element_type=jnp.float32)
    column = jnp.broadcast_to(scale[...], (8, scale.shape[1])).T[:, :1]
    stacked[padded - 8 : padded, :] = jnp.zeros((8, count), jnp.float32)
    stacked[:classes, :] = coefficients[...]
    weights[...] = total
    for x in range(lax.axis_size(X)):
        at = pl.multiple_of((x * groups + lax.axis_index(Y)) * split, split)
        stacked[padded + x * split : padded + (x + 1) * split, :] = weights[pl.ds(at, split), :]
    high[...], low[...] = in_two(stacked[...])
    weights[...] = total * (step_rate * column)


def add(own, other, total):
    total[...] = own[...] + other[...]


def join(own, other, copies, *, classes):
    total = own[...] + other[...]
    _, lanes = total.shape
    lane = lax.broadcasted_iota(jnp.int32, total.shape, 1)
    total = jnp.where(lane < classes, total, 0.0)
    largest = jnp.maximum(jnp.max(jnp.abs(total), axis=1, keepdims=True), 1e-30)
    power = jnp.clip(jnp.ceil(jnp.log2(largest)), -100.0, 100.0)
    factor = jnp.ceil(largest * jnp.exp2(-power) * 16384.0) + 1.0
    steps = jnp.floor(total * (CODES / (factor * jnp.exp2(power) / 16384.0)) + 0.5)
    steps = jnp.clip(steps, -CODES, CODES)
    steps = jnp.where(lane == lanes - 2, factor, jnp.where(lane == lanes - 1, power, steps))
    codes = steps.astype(jnp.int32).astype(jnp.int16)
    copies[...] = jnp.broadcast_to(codes[None], copies.shape)


def decoded(codes):
    steps = codes.astype(jnp.int32).astype(jnp.float32)
    lanes = steps.shape[1]
    lane = lax.broadcasted_iota(jnp.int32, steps.shape, 1)
    pick = lambda n: jnp.sum(jnp.where(lane == n, steps, 0.0), axis=1, keepdims=True)
    return steps * (pick(lanes - 2) * jnp.exp2(pick(lanes - 1)) / 16384.0 / CODES)


def targets_of(labels, j, rows, classes):
    ids = lax.broadcasted_iota(jnp.int32, (rows, 2 * LANES), 0) + lax.axis_index(Y) * classes
    return (labels[j] == ids).astype(jnp.float32)


def project(own, first, second, third, fourth, labels, projected, *, classes, rows_each):
    blocks, split, lanes = first.shape
    rows = own.shape[1]
    groups = projected.shape[0] // split
    pieces = (first, second, third, fourth)[:groups]
    side = 1 - lax.axis_index(K)
    spot = lax.broadcasted_iota(jnp.int32, (lanes, 2 * lanes), 0)
    lane = lax.broadcasted_iota(jnp.int32, (lanes, 2 * lanes), 1)
    line = spot // rows_each * (2 * rows_each) + side * rows_each + spot % rows_each
    picks = (lane == line).astype(jnp.float32).astype(jnp.bfloat16)
    total = jnp.zeros(projected.shape, jnp.float32)
    for t in range(0, blocks, 2):
        lines = [jnp.concatenate([p[t], p[t + 1]], axis=1) for p in pieces]
        gradient = []
        for j in (t, t + 1):
            targets = targets_of(labels, j, rows, classes).astype(jnp.bfloat16)
            hits = lax.dot_general(targets, picks, LAST, preferred_element_type=jnp.float32)
            gradient.append(own[j] - hits)
        total += product(
            in_two(jnp.concatenate(lines, axis=0)),
            in_two(jnp.concatenate(gradient, axis=1)),
            LAST,
        )
    for s in range(groups):
        at = pl.multiple_of(lax.rem(lax.axis_index(Y) + s, groups) * split, split)
        projected[pl.ds(at, split), :] = total[s * split : (s + 1) * split]


def step_batch(own, other, labels, index, coefficients, output, updated, *, rows_each):
    blocks, rows, lanes = own.shape
    classes, count = coefficients.shape
    total = jnp.zeros((rows, count), jnp.float32)
    slots = lax.broadcasted_iota(jnp.int32, (count, 2 * lanes), 0)
    slots += lax.axis_index(ROWS) * count
    spot = lax.broadcasted_iota(jnp.int32, (2 * lanes, 2 * lanes), 0)
    lane = lax.broadcasted_iota(jnp.int32, (2 * lanes, 2 * lanes), 1)
    core = jnp.where(spot < lanes, 1 - lax.axis_index(K), lax.axis_index(K))
    place = spot % lanes
    line = place // rows_each * (2 * rows_each) + core * rows_each + place % rows_each
    picks = (lane == line).astype(jnp.float32).astype(jnp.bfloat16)
    for j in range(blocks):
        rest = jnp.concatenate([own[j], other[j]], axis=1)
        predicted = jnp.zeros((rows, 2 * lanes), jnp.float32)
        for _ in range(3):
            part = rest.astype(jnp.bfloat16)
            predicted += jnp.dot(part, picks, preferred_element_type=jnp.float32)
            rest = rest - part.astype(jnp.float32)
        output[:, 2 * j * lanes : 2 * (j + 1) * lanes] = predicted[:classes]
        hits = (index[j] == slots).astype(jnp.float32).astype(jnp.bfloat16)
        for part in in_two(predicted - targets_of(labels, j, rows, classes)):
            total += lax.dot_general(part, hits, LAST, preferred_element_type=jnp.float32)
    updated[...] = coefficients[...] - step_rate * total[:classes]


def correct(updated, projected, weights, result):
    classes = updated.shape[0]
    change = product(in_two(decoded(projected[...])), in_two(weights[...]), FIRST)
    result[...] = updated[...] + change[:classes]


def kernel(body, outs, scratch=(), limit=16, **settings):
    near = pl.BlockSpec(memory_space=pltpu.VMEM)

    def call(*operands):
        return pl.pallas_call(
            functools.partial(body, **settings),
            out_shape=outs,
            in_specs=[near for _ in operands],
            out_specs=jax.tree.map(lambda _: near, outs),
            scratch_shapes=scratch,
            compiler_params=pltpu.CompilerParams(vmem_limit_bytes=limit * 2**20),
            interpret=INTERPRET,
        )(*operands)

    return call


def from_others(value, axis):
    size = lax.axis_size(axis)
    pieces = [value]
    for s in range(1, size):
        pieces.append(lax.ppermute(value, axis, [((d + s) % size, d) for d in range(size)]))
    return pieces + [value] * (4 - size)


def shards(
    centers,
    coefficients,
    batch_features,
    batch_labels,
    batch_index,
    subset_index,
    eigen_vectors,
    eigen_scale,
):
    depth, chips, groups = (lax.axis_size(a) for a in (Z, X, Y))
    count = centers.shape[0]
    classes = coefficients.shape[0]
    vectors = eigen_vectors.shape[1]
    split = vectors // groups // chips
    padded = -(-classes // 8) * 8
    while padded < classes + 2 or (padded + vectors // groups) % (8 * depth):
        padded += 8
    lines = padded + vectors // groups
    batch = batch_labels.shape[0]
    array = lambda *shape: jax.ShapeDtypeStruct(shape, jnp.float32)

    batch_own = lax.all_to_all(
        kernel(
            fan, jax.ShapeDtypeStruct((depth, *batch_features.shape), batch_features.dtype), limit=2
        )(batch_features),
        Z,
        0,
        0,
        tiled=True,
    )
    batch_own, turned = lax.optimization_barrier((batch_own, centers.T))
    center_pieces = from_others(turned, Y)
    rows, width = batch_features.shape
    granules = (depth * (2 * width // LANES) // 2, rows, LANES)
    copies = kernel(
        pack,
        jax.ShapeDtypeStruct((chips * groups, *granules), batch_own.dtype),
        (pltpu.VMEM(granules, batch_own.dtype),),
        limit=2,
    )(batch_own)
    batch_own = lax.all_to_all(copies, (X, Y), 0, 0, tiled=True)
    batch_own, center_pieces = lax.optimization_barrier((batch_own, center_pieces))
    batch_own = batch_own.reshape(chips, groups, *granules)
    batch_other = from_others(batch_own, K)[1]

    high, low, weights = kernel(
        lift,
        (
            jax.ShapeDtypeStruct((lines, count), jnp.bfloat16),
            jax.ShapeDtypeStruct((lines, count), jnp.bfloat16),
            array(vectors, count),
        ),
        (pltpu.VMEM((lines, count), jnp.float32),),
        limit=6,
    )(eigen_vectors, eigen_scale[None], subset_index[None], coefficients)
    labels = batch_labels.reshape(chips, 1, 2 * LANES)
    index = batch_index.reshape(chips, 1, 2 * LANES)

    products = kernel(kernel_products, array(chips, lines, LANES), limit=12, padded=padded)
    sent = from_others(products(batch_own, *center_pieces, high, low), K)[1]
    kept = products(batch_other, *center_pieces, high, low)
    own = kernel(add, array(chips, lines, LANES), limit=6)(kept, sent)

    own = scattered(own, X)
    own = scattered(own.reshape(depth, lines // depth, LANES), Z)
    own = gathered(own, Z).reshape(lines, LANES)
    copies, basis = kernel(
        part, (array(chips, padded, LANES), array(chips, split, LANES)), limit=4
    )(own)
    basis = from_others(basis, Y)
    predicted = lax.all_to_all(copies, X, 0, 0, tiled=True)
    predicted, basis = lax.optimization_barrier((predicted, basis))

    half = kernel(
        project, array(groups * split, padded), classes=classes, rows_each=rows
    )(predicted, *basis, labels)
    codes = jax.ShapeDtypeStruct((chips, groups * split, padded), jnp.int16)
    copies = kernel(join, codes, limit=4, classes=classes)(
        *from_others(half, K)[:2]
    )
    copies, late = lax.optimization_barrier((copies, predicted))
    projected = lax.all_to_all(copies, X, 0, 0, tiled=True).reshape(vectors, padded)

    late = from_others(late, K)[:2]
    output, updated = kernel(
        step_batch, (array(classes, batch), array(classes, count)), rows_each=rows
    )(*late, labels, index, coefficients)
    result = kernel(correct, array(classes, count))(updated, projected, weights)
    return (output, result)


def solution(mesh, shape=(16, 4, 2)):
    finer = Mesh(mesh.devices.reshape(*shape, mesh.shape["cls"]), (*ROWS, Y))
    placed = (P(ROWS, Y), P(Y, ROWS), P(ROWS, Y), P(), P(), P(ROWS), P(ROWS, None), P())

    return jax.shard_map(
        shards,
        mesh=finer,
        in_specs=placed,
        out_specs=(P(Y, None), P(Y, ROWS)),
        check_vma=False,
    )
```

```python
import functools

import jax
import jax.numpy as jnp
from jax import lax
from jax.experimental import pallas as pl
from jax.experimental.pallas import tpu as pltpu
from jax.sharding import Mesh
from jax.sharding import PartitionSpec as P


Z, X, K, Y = "rows_z", "rows_x", "rows_k", "cls"
ROWS = (Z, X, K)
LANES = 128
INTERPRET = False

CODES = 32767.0

spread = 4.0
step_rate = 0.5

LAST = (((1,), (1,)), ((), ()))
FIRST = (((0,), (0,)), ((), ()))


def gathered(value, axis):
    copies = jnp.broadcast_to(value, (lax.axis_size(axis), *value.shape))
    return lax.all_to_all(copies, axis, 0, 0, tiled=True)


def scattered(tiles, axis):
    return jnp.sum(lax.all_to_all(tiles, axis, 0, 0, tiled=True), axis=0)


def in_two(value):
    high = value.astype(jnp.bfloat16)
    low = (value - high.astype(jnp.float32)).astype(jnp.bfloat16)
    return high, low


def product(left, right, dims):
    (a, b), (c, d) = left, right
    one = lambda u, v: lax.dot_general(u, v, dims, preferred_element_type=jnp.float32)
    return one(a, d) + one(b, c) + one(a, c)


def fan(value, copies):
    copies[...] = jnp.broadcast_to(value[...][None], copies.shape)


def part(sums, copies, basis):
    padded = copies.shape[1]
    copies[...] = jnp.broadcast_to(sums[:padded][None], copies.shape)
    basis[...] = sums[padded:].reshape(basis.shape)


def pack(batch, copies, granules):
    depth, _, width = batch.shape
    full, rest = width // LANES, width % LANES
    half = depth // 2
    for z in range(depth):
        for h in range(full):
            granules[z * full + h] = batch[z, :, h * LANES : (h + 1) * LANES]
    for z in range(half):
        at = depth * full + z
        granules[at, :, :rest] = batch[z, :, full * LANES :]
        granules[at, :, rest:] = batch[z + half, :, full * LANES :]
    copies[...] = jnp.broadcast_to(granules[...][None], copies.shape)


def kernel_products(batch, first, second, third, fourth, high, low, sums, *, padded):
    chips, groups, granules, _, lanes = batch.shape
    blocks, lines, _ = sums.shape
    count = high.shape[1]
    full, rest = first.shape[0] // lanes, first.shape[0] % lanes
    depth = 2 * granules // (2 * full + 1)
    half = depth // 2
    near = depth // blocks
    split = (lines - padded) // blocks
    centers = (first, second, third, fourth)[:groups]

    center_norm = jnp.zeros((1, count), jnp.float32)
    tails = []
    for piece in centers:
        wide = piece[...].astype(jnp.float32)
        center_norm += jnp.sum(wide * wide, axis=0, keepdims=True)
        tails.append(piece[full * lanes :])
    none = jnp.zeros((rest, count), tails[0].dtype)
    low_tail = jnp.concatenate([v for t in tails for v in (t, none)], axis=0)
    high_tail = jnp.concatenate([v for t in tails for v in (none, t)], axis=0)
    lane = lax.broadcasted_iota(jnp.int32, (2 * lanes, lanes), 1)

    for t in range(0, blocks, 2):
        inner = jnp.zeros((2 * lanes, count), jnp.float32)
        batch_norm = jnp.zeros((2 * lanes, 1), jnp.float32)
        is_high = t * near >= half
        is_own = (lane >= rest) if is_high else (lane < rest)
        ends = []
        for s in range(groups):
            y = lax.rem(lax.axis_index(Y) + s, groups)
            columns = []
            for h in range(full + 1):
                pieces = []
                for z in range(t * near, (t + 2) * near):
                    at = z * full + h if h < full else depth * full + z % half
                    pieces += [batch[x, y, at] for x in range(chips)]
                columns.append(jnp.concatenate(pieces, axis=0))
                wide = columns[h].astype(jnp.float32)
                wide = wide if h < full else jnp.where(is_own, wide, 0.0)
                batch_norm += jnp.sum(wide * wide, axis=1, keepdims=True)
            ends.append(columns.pop())
            inner += jnp.dot(
                jnp.concatenate(columns, axis=1),
                centers[s][: full * lanes],
                preferred_element_type=jnp.float32,
            )
        inner += jnp.dot(
            jnp.concatenate(ends, axis=1),
            high_tail if is_high else low_tail,
            preferred_element_type=jnp.float32,
        )
        squared = center_norm + batch_norm - 2.0 * inner
        values = jnp.exp(-jnp.sqrt(jnp.maximum(squared, 0.0)) / spread)
        out = product((high[...], low[...]), in_two(values), LAST)
        for j in range(2):
            part = out[:, j * lanes : (j + 1) * lanes]
            sums[t + j, :padded, :] = part[:padded]
            at = padded + (t + j) * split
            sums[:, at : at + split, :] = part[padded:].reshape(blocks, split, lanes)


def lift(vectors, scale, index, coefficients, high, low, weights, stacked):
    classes, count = coefficients.shape
    lines, groups = stacked.shape[0], lax.axis_size(Y)
    own = weights.shape[0] // groups
    padded = lines - own
    split = own // lax.axis_size(X)
    slots = lax.broadcasted_iota(jnp.int32, (count, index.shape[1]), 0)
    hits = index[...] == slots + lax.axis_index(ROWS) * count
    hits = hits.astype(jnp.float32).astype(jnp.bfloat16)
    turned = vectors[...].T
    total = jnp.zeros(weights.shape, jnp.float32)
    for part in in_two(turned):
        total += lax.dot_general(part, hits, LAST, preferred_element_type=jnp.float32)
    column = jnp.broadcast_to(scale[...], (8, scale.shape[1])).T[:, :1]
    stacked[padded - 8 : padded, :] = jnp.zeros((8, count), jnp.float32)
    stacked[:classes, :] = coefficients[...]
    weights[...] = total
    for x in range(lax.axis_size(X)):
        at = pl.multiple_of((x * groups + lax.axis_index(Y)) * split, split)
        stacked[padded + x * split : padded + (x + 1) * split, :] = weights[pl.ds(at, split), :]
    high[...], low[...] = in_two(stacked[...])
    weights[...] = total * (step_rate * column)


def add(own, other, total):
    total[...] = own[...] + other[...]


def join(own, other, copies, *, classes):
    total = own[...] + other[...]
    _, lanes = total.shape
    lane = lax.broadcasted_iota(jnp.int32, total.shape, 1)
    total = jnp.where(lane < classes, total, 0.0)
    largest = jnp.maximum(jnp.max(jnp.abs(total), axis=1, keepdims=True), 1e-30)
    power = jnp.clip(jnp.ceil(jnp.log2(largest)), -100.0, 100.0)
    factor = jnp.ceil(largest * jnp.exp2(-power) * 16384.0) + 1.0
    steps = jnp.floor(total * (CODES / (factor * jnp.exp2(power) / 16384.0)) + 0.5)
    steps = jnp.clip(steps, -CODES, CODES)
    steps = jnp.where(lane == lanes - 2, factor, jnp.where(lane == lanes - 1, power, steps))
    codes = steps.astype(jnp.int32).astype(jnp.int16)
    copies[...] = jnp.broadcast_to(codes[None], copies.shape)


def decoded(codes):
    steps = codes.astype(jnp.int32).astype(jnp.float32)
    lanes = steps.shape[1]
    lane = lax.broadcasted_iota(jnp.int32, steps.shape, 1)
    pick = lambda n: jnp.sum(jnp.where(lane == n, steps, 0.0), axis=1, keepdims=True)
    return steps * (pick(lanes - 2) * jnp.exp2(pick(lanes - 1)) / 16384.0 / CODES)


def targets_of(labels, j, rows, classes):
    ids = lax.broadcasted_iota(jnp.int32, (rows, 2 * LANES), 0) + lax.axis_index(Y) * classes
    return (labels[j] == ids).astype(jnp.float32)


def project(own, first, second, third, fourth, labels, projected, *, classes, rows_each):
    blocks, split, lanes = first.shape
    rows = own.shape[1]
    groups = projected.shape[0] // split
    pieces = (first, second, third, fourth)[:groups]
    side = 1 - lax.axis_index(K)
    spot = lax.broadcasted_iota(jnp.int32, (lanes, 2 * lanes), 0)
    lane = lax.broadcasted_iota(jnp.int32, (lanes, 2 * lanes), 1)
    line = spot // rows_each * (2 * rows_each) + side * rows_each + spot % rows_each
    picks = (lane == line).astype(jnp.float32).astype(jnp.bfloat16)
    total = jnp.zeros(projected.shape, jnp.float32)
    for t in range(0, blocks, 2):
        lines = [jnp.concatenate([p[t], p[t + 1]], axis=1) for p in pieces]
        gradient = []
        for j in (t, t + 1):
            targets = targets_of(labels, j, rows, classes).astype(jnp.bfloat16)
            hits = lax.dot_general(targets, picks, LAST, preferred_element_type=jnp.float32)
            gradient.append(own[j] - hits)
        total += product(
            in_two(jnp.concatenate(lines, axis=0)),
            in_two(jnp.concatenate(gradient, axis=1)),
            LAST,
        )
    for s in range(groups):
        at = pl.multiple_of(lax.rem(lax.axis_index(Y) + s, groups) * split, split)
        projected[pl.ds(at, split), :] = total[s * split : (s + 1) * split]


def step_batch(own, other, labels, index, coefficients, output, updated, *, rows_each):
    blocks, rows, lanes = own.shape
    classes, count = coefficients.shape
    total = jnp.zeros((rows, count), jnp.float32)
    slots = lax.broadcasted_iota(jnp.int32, (count, 2 * lanes), 0)
    slots += lax.axis_index(ROWS) * count
    spot = lax.broadcasted_iota(jnp.int32, (2 * lanes, 2 * lanes), 0)
    lane = lax.broadcasted_iota(jnp.int32, (2 * lanes, 2 * lanes), 1)
    core = jnp.where(spot < lanes, 1 - lax.axis_index(K), lax.axis_index(K))
    place = spot % lanes
    line = place // rows_each * (2 * rows_each) + core * rows_each + place % rows_each
    picks = (lane == line).astype(jnp.float32).astype(jnp.bfloat16)
    for j in range(blocks):
        rest = jnp.concatenate([own[j], other[j]], axis=1)
        predicted = jnp.zeros((rows, 2 * lanes), jnp.float32)
        for _ in range(3):
            part = rest.astype(jnp.bfloat16)
            predicted += jnp.dot(part, picks, preferred_element_type=jnp.float32)
            rest = rest - part.astype(jnp.float32)
        output[:, 2 * j * lanes : 2 * (j + 1) * lanes] = predicted[:classes]
        hits = (index[j] == slots).astype(jnp.float32).astype(jnp.bfloat16)
        for part in in_two(predicted - targets_of(labels, j, rows, classes)):
            total += lax.dot_general(part, hits, LAST, preferred_element_type=jnp.float32)
    updated[...] = coefficients[...] - step_rate * total[:classes]


def correct(updated, projected, weights, result):
    classes = updated.shape[0]
    change = product(in_two(decoded(projected[...])), in_two(weights[...]), FIRST)
    result[...] = updated[...] + change[:classes]


def kernel(body, outs, scratch=(), limit=16, **settings):
    near = pl.BlockSpec(memory_space=pltpu.VMEM)

    def call(*operands):
        return pl.pallas_call(
            functools.partial(body, **settings),
            out_shape=outs,
            in_specs=[near for _ in operands],
            out_specs=jax.tree.map(lambda _: near, outs),
            scratch_shapes=scratch,
            compiler_params=pltpu.CompilerParams(vmem_limit_bytes=limit * 2**20),
            interpret=INTERPRET,
        )(*operands)

    return call


def from_others(value, axis):
    size = lax.axis_size(axis)
    pieces = [value]
    for s in range(1, size):
        pairs = [((d + s) % size, d) for d in range(size)]
        pieces.append(lax.ppermute(value, axis, pairs))
    return pieces + [value] * (4 - size)


def shards(
    centers,
    coefficients,
    batch_features,
    batch_labels,
    batch_index,
    subset_index,
    eigen_vectors,
    eigen_scale,
):
    depth, chips, groups = (lax.axis_size(a) for a in (Z, X, Y))
    count = centers.shape[0]
    classes = coefficients.shape[0]
    vectors = eigen_vectors.shape[1]
    split = vectors // groups // chips
    padded = -(-classes // 8) * 8
    while padded < classes + 2 or (padded + vectors // groups) % (8 * depth):
        padded += 8
    lines = padded + vectors // groups
    batch = batch_labels.shape[0]
    array = lambda *shape: jax.ShapeDtypeStruct(shape, jnp.float32)

    batch_own = lax.all_to_all(
        kernel(
            fan, jax.ShapeDtypeStruct((depth, *batch_features.shape), batch_features.dtype), limit=2
        )(batch_features),
        Z,
        0,
        0,
        tiled=True,
    )
    turned = centers.T
    center_pieces = from_others(turned, Y)
    rows, width = batch_features.shape
    granules = (depth * (2 * width // LANES) // 2, rows, LANES)
    copies = kernel(
        pack,
        jax.ShapeDtypeStruct((chips * groups, *granules), batch_own.dtype),
        (pltpu.VMEM(granules, batch_own.dtype),),
        limit=2,
    )(batch_own)
    batch_own = lax.all_to_all(copies, (X, Y), 0, 0, tiled=True)
    high, low, weights = kernel(
        lift,
        (
            jax.ShapeDtypeStruct((lines, count), jnp.bfloat16),
            jax.ShapeDtypeStruct((lines, count), jnp.bfloat16),
            array(vectors, count),
        ),
        (pltpu.VMEM((lines, count), jnp.float32),),
        limit=6,
    )(eigen_vectors, eigen_scale[None], subset_index[None], coefficients)
    batch_own, center_pieces, high, low, weights = lax.optimization_barrier(
        (batch_own, center_pieces, high, low, weights)
    )
    batch_own = batch_own.reshape(chips, groups, *granules)
    batch_other = from_others(batch_own, K)[1]

    labels = batch_labels.reshape(chips, 1, 2 * LANES)
    index = batch_index.reshape(chips, 1, 2 * LANES)

    products = kernel(kernel_products, array(chips, lines, LANES), limit=12, padded=padded)
    sent = from_others(products(batch_own, *center_pieces, high, low), K)[1]
    kept = products(batch_other, *center_pieces, high, low)
    own = kernel(add, array(chips, lines, LANES), limit=6)(kept, sent)

    own = scattered(own, X)
    own = scattered(own.reshape(depth, lines // depth, LANES), Z)
    own = gathered(own, Z).reshape(lines, LANES)
    copies, basis = kernel(
        part, (array(chips, padded, LANES), array(chips, split, LANES)), limit=4
    )(own)
    basis = from_others(basis, Y)
    predicted = lax.all_to_all(copies, X, 0, 0, tiled=True)
    predicted, basis = lax.optimization_barrier((predicted, basis))

    half = kernel(
        project, array(groups * split, padded), classes=classes, rows_each=rows
    )(predicted, *basis, labels)
    codes = jax.ShapeDtypeStruct((chips, groups * split, padded), jnp.int16)
    copies = kernel(join, codes, limit=4, classes=classes)(
        *from_others(half, K)[:2]
    )
    copies, late = lax.optimization_barrier((copies, predicted))
    projected = lax.all_to_all(copies, X, 0, 0, tiled=True).reshape(vectors, padded)

    late = from_others(late, K)[:2]
    output, updated = kernel(
        step_batch, (array(classes, batch), array(classes, count)), rows_each=rows
    )(*late, labels, index, coefficients)
    result = kernel(correct, array(classes, count))(updated, projected, weights)
    return (output, result)


def solution(mesh, shape=(16, 4, 2)):
    finer = Mesh(mesh.devices.reshape(*shape, mesh.shape["cls"]), (*ROWS, Y))
    placed = (P(ROWS, Y), P(Y, ROWS), P(ROWS, Y), P(), P(), P(ROWS), P(ROWS, None), P())

    return jax.shard_map(
        shards,
        mesh=finer,
        in_specs=placed,
        out_specs=(P(Y, None), P(Y, ROWS)),
        check_vma=False,
    )
```

```python
import functools

import jax
import jax.numpy as jnp
from jax import lax
from jax.experimental import pallas as pl
from jax.experimental.pallas import tpu as pltpu
from jax.sharding import Mesh
from jax.sharding import PartitionSpec as P


Z, X, K, Y = "rows_z", "rows_x", "rows_k", "cls"
ROWS = (Z, X, K)
LANES = 128
INTERPRET = False

CODES = 32767.0

spread = 4.0
step_rate = 0.5

LAST = (((1,), (1,)), ((), ()))
FIRST = (((0,), (0,)), ((), ()))


def gathered(value, axis):
    copies = jnp.broadcast_to(value, (lax.axis_size(axis), *value.shape))
    return lax.all_to_all(copies, axis, 0, 0, tiled=True)


def scattered(tiles, axis):
    return jnp.sum(lax.all_to_all(tiles, axis, 0, 0, tiled=True), axis=0)


def in_two(value):
    high = value.astype(jnp.bfloat16)
    low = (value - high.astype(jnp.float32)).astype(jnp.bfloat16)
    return high, low


def product(left, right, dims):
    (a, b), (c, d) = left, right
    one = lambda u, v: lax.dot_general(u, v, dims, preferred_element_type=jnp.float32)
    return one(a, d) + one(b, c) + one(a, c)


def fan(value, copies):
    copies[...] = jnp.broadcast_to(value[...][None], copies.shape)


def part(sums, copies, basis):
    padded = copies.shape[1]
    copies[...] = jnp.broadcast_to(sums[:padded][None], copies.shape)
    basis[...] = sums[padded:].reshape(basis.shape)


def pack(batch, copies, granules):
    depth, _, width = batch.shape
    full, rest = width // LANES, width % LANES
    half = depth // 2
    for z in range(depth):
        for h in range(full):
            granules[z * full + h] = batch[z, :, h * LANES : (h + 1) * LANES]
    for z in range(half):
        at = depth * full + z
        granules[at, :, :rest] = batch[z, :, full * LANES :]
        granules[at, :, rest:] = batch[z + half, :, full * LANES :]
    copies[...] = jnp.broadcast_to(granules[...][None], copies.shape)


def kernel_products(batch, first, second, third, fourth, high, low, sums, *, padded):
    chips, groups, granules, _, lanes = batch.shape
    blocks, lines, _ = sums.shape
    count = high.shape[1]
    full, rest = first.shape[0] // lanes, first.shape[0] % lanes
    depth = 2 * granules // (2 * full + 1)
    half = depth // 2
    near = depth // blocks
    split = (lines - padded) // blocks
    centers = (first, second, third, fourth)[:groups]

    center_norm = jnp.zeros((1, count), jnp.float32)
    tails = []
    for piece in centers:
        wide = piece[...].astype(jnp.float32)
        center_norm += jnp.sum(wide * wide, axis=0, keepdims=True)
        tails.append(piece[full * lanes :])
    none = jnp.zeros((rest, count), tails[0].dtype)
    low_tail = jnp.concatenate([v for t in tails for v in (t, none)], axis=0)
    high_tail = jnp.concatenate([v for t in tails for v in (none, t)], axis=0)
    lane = lax.broadcasted_iota(jnp.int32, (2 * lanes, lanes), 1)

    for t in range(0, blocks, 2):
        inner = jnp.zeros((2 * lanes, count), jnp.float32)
        batch_norm = jnp.zeros((2 * lanes, 1), jnp.float32)
        is_high = t * near >= half
        is_own = (lane >= rest) if is_high else (lane < rest)
        ends = []
        for s in range(groups):
            y = lax.rem(lax.axis_index(Y) + s, groups)
            columns = []
            for h in range(full + 1):
                pieces = []
                for z in range(t * near, (t + 2) * near):
                    at = z * full + h if h < full else depth * full + z % half
                    pieces += [batch[x, y, at] for x in range(chips)]
                columns.append(jnp.concatenate(pieces, axis=0))
                wide = columns[h].astype(jnp.float32)
                wide = wide if h < full else jnp.where(is_own, wide, 0.0)
                batch_norm += jnp.sum(wide * wide, axis=1, keepdims=True)
            ends.append(columns.pop())
            inner += jnp.dot(
                jnp.concatenate(columns, axis=1),
                centers[s][: full * lanes],
                preferred_element_type=jnp.float32,
            )
        inner += jnp.dot(
            jnp.concatenate(ends, axis=1),
            high_tail if is_high else low_tail,
            preferred_element_type=jnp.float32,
        )
        squared = center_norm + batch_norm - 2.0 * inner
        values = jnp.exp(-jnp.sqrt(jnp.maximum(squared, 0.0)) / spread)
        out = product((high[...], low[...]), in_two(values), LAST)
        for j in range(2):
            part = out[:, j * lanes : (j + 1) * lanes]
            sums[t + j, :padded, :] = part[:padded]
            at = padded + (t + j) * split
            sums[:, at : at + split, :] = part[padded:].reshape(blocks, split, lanes)


def lift(vectors, scale, index, coefficients, high, low, weights, stacked):
    classes, count = coefficients.shape
    lines, groups = stacked.shape[0], lax.axis_size(Y)
    own = weights.shape[0] // groups
    padded = lines - own
    split = own // lax.axis_size(X)
    slots = lax.broadcasted_iota(jnp.int32, (count, index.shape[1]), 0)
    hits = index[...] == slots + lax.axis_index(ROWS) * count
    hits = hits.astype(jnp.float32).astype(jnp.bfloat16)
    turned = vectors[...].T
    total = jnp.zeros(weights.shape, jnp.float32)
    for part in in_two(turned):
        total += lax.dot_general(part, hits, LAST, preferred_element_type=jnp.float32)
    column = jnp.broadcast_to(scale[...], (8, scale.shape[1])).T[:, :1]
    stacked[padded - 8 : padded, :] = jnp.zeros((8, count), jnp.float32)
    stacked[:classes, :] = coefficients[...]
    weights[...] = total
    for x in range(lax.axis_size(X)):
        at = pl.multiple_of((x * groups + lax.axis_index(Y)) * split, split)
        stacked[padded + x * split : padded + (x + 1) * split, :] = weights[pl.ds(at, split), :]
    high[...], low[...] = in_two(stacked[...])
    weights[...] = total * (step_rate * column)


def add(own, other, total):
    total[...] = own[...] + other[...]


def join(own, other, copies, *, classes):
    total = own[...] + other[...]
    _, lanes = total.shape
    lane = lax.broadcasted_iota(jnp.int32, total.shape, 1)
    total = jnp.where(lane < classes, total, 0.0)
    largest = jnp.maximum(jnp.max(jnp.abs(total), axis=1, keepdims=True), 1e-30)
    power = jnp.clip(jnp.ceil(jnp.log2(largest)), -100.0, 100.0)
    factor = jnp.ceil(largest * jnp.exp2(-power) * 16384.0) + 1.0
    steps = jnp.floor(total * (CODES / (factor * jnp.exp2(power) / 16384.0)) + 0.5)
    steps = jnp.clip(steps, -CODES, CODES)
    steps = jnp.where(lane == lanes - 2, factor, jnp.where(lane == lanes - 1, power, steps))
    codes = steps.astype(jnp.int32).astype(jnp.int16)
    copies[...] = jnp.broadcast_to(codes[None], copies.shape)


def decoded(codes):
    steps = codes.astype(jnp.int32).astype(jnp.float32)
    lanes = steps.shape[1]
    lane = lax.broadcasted_iota(jnp.int32, steps.shape, 1)
    pick = lambda n: jnp.sum(jnp.where(lane == n, steps, 0.0), axis=1, keepdims=True)
    return steps * (pick(lanes - 2) * jnp.exp2(pick(lanes - 1)) / 16384.0 / CODES)


def targets_of(labels, j, rows, classes):
    ids = lax.broadcasted_iota(jnp.int32, (rows, 2 * LANES), 0) + lax.axis_index(Y) * classes
    return (labels[j] == ids).astype(jnp.float32)


def project(own, first, second, third, fourth, labels, projected, *, classes, rows_each):
    blocks, split, lanes = first.shape
    rows = own.shape[1]
    groups = projected.shape[0] // split
    pieces = (first, second, third, fourth)[:groups]
    side = 1 - lax.axis_index(K)
    spot = lax.broadcasted_iota(jnp.int32, (lanes, 2 * lanes), 0)
    lane = lax.broadcasted_iota(jnp.int32, (lanes, 2 * lanes), 1)
    line = spot // rows_each * (2 * rows_each) + side * rows_each + spot % rows_each
    picks = (lane == line).astype(jnp.float32).astype(jnp.bfloat16)
    total = jnp.zeros(projected.shape, jnp.float32)
    for t in range(0, blocks, 2):
        lines = [jnp.concatenate([p[t], p[t + 1]], axis=1) for p in pieces]
        gradient = []
        for j in (t, t + 1):
            targets = targets_of(labels, j, rows, classes).astype(jnp.bfloat16)
            hits = lax.dot_general(targets, picks, LAST, preferred_element_type=jnp.float32)
            gradient.append(own[j] - hits)
        total += product(
            in_two(jnp.concatenate(lines, axis=0)),
            in_two(jnp.concatenate(gradient, axis=1)),
            LAST,
        )
    for s in range(groups):
        at = pl.multiple_of(lax.rem(lax.axis_index(Y) + s, groups) * split, split)
        projected[pl.ds(at, split), :] = total[s * split : (s + 1) * split]


def step_batch(own, other, labels, index, coefficients, output, updated, *, rows_each):
    blocks, rows, lanes = own.shape
    classes, count = coefficients.shape
    total = jnp.zeros((rows, count), jnp.float32)
    slots = lax.broadcasted_iota(jnp.int32, (count, 2 * lanes), 0)
    slots += lax.axis_index(ROWS) * count
    spot = lax.broadcasted_iota(jnp.int32, (2 * lanes, 2 * lanes), 0)
    lane = lax.broadcasted_iota(jnp.int32, (2 * lanes, 2 * lanes), 1)
    core = jnp.where(spot < lanes, 1 - lax.axis_index(K), lax.axis_index(K))
    place = spot % lanes
    line = place // rows_each * (2 * rows_each) + core * rows_each + place % rows_each
    picks = (lane == line).astype(jnp.float32).astype(jnp.bfloat16)
    for j in range(blocks):
        rest = jnp.concatenate([own[j], other[j]], axis=1)
        predicted = jnp.zeros((rows, 2 * lanes), jnp.float32)
        for _ in range(3):
            part = rest.astype(jnp.bfloat16)
            predicted += jnp.dot(part, picks, preferred_element_type=jnp.float32)
            rest = rest - part.astype(jnp.float32)
        output[:, 2 * j * lanes : 2 * (j + 1) * lanes] = predicted[:classes]
        hits = (index[j] == slots).astype(jnp.float32).astype(jnp.bfloat16)
        for part in in_two(predicted - targets_of(labels, j, rows, classes)):
            total += lax.dot_general(part, hits, LAST, preferred_element_type=jnp.float32)
    updated[...] = coefficients[...] - step_rate * total[:classes]


def correct(updated, projected, weights, result):
    classes = updated.shape[0]
    change = product(in_two(decoded(projected[...])), in_two(weights[...]), FIRST)
    result[...] = updated[...] + change[:classes]


def kernel(body, outs, scratch=(), limit=16, **settings):
    near = pl.BlockSpec(memory_space=pltpu.VMEM)

    def call(*operands):
        return pl.pallas_call(
            functools.partial(body, **settings),
            out_shape=outs,
            in_specs=[near for _ in operands],
            out_specs=jax.tree.map(lambda _: near, outs),
            scratch_shapes=scratch,
            compiler_params=pltpu.CompilerParams(vmem_limit_bytes=limit * 2**20),
            interpret=INTERPRET,
        )(*operands)

    return call


def from_others(value, axis):
    size = lax.axis_size(axis)
    pieces = [value]
    for s in range(1, size):
        pairs = [((d + s) % size, d) for d in range(size)]
        pieces.append(lax.ppermute(value, axis, pairs))
    return pieces + [value] * (4 - size)


def shards(
    centers,
    coefficients,
    batch_features,
    batch_labels,
    batch_index,
    subset_index,
    eigen_vectors,
    eigen_scale,
):
    depth, chips, groups = (lax.axis_size(a) for a in (Z, X, Y))
    count = centers.shape[0]
    classes = coefficients.shape[0]
    vectors = eigen_vectors.shape[1]
    split = vectors // groups // chips
    padded = -(-classes // 8) * 8
    while padded < classes + 2 or (padded + vectors // groups) % (8 * depth):
        padded += 8
    lines = padded + vectors // groups
    batch = batch_labels.shape[0]
    array = lambda *shape: jax.ShapeDtypeStruct(shape, jnp.float32)

    batch_own = lax.all_to_all(
        kernel(
            fan, jax.ShapeDtypeStruct((depth, *batch_features.shape), batch_features.dtype), limit=2
        )(batch_features),
        Z,
        0,
        0,
        tiled=True,
    )
    turned = centers.T
    center_pieces = from_others(turned, Y)
    rows, width = batch_features.shape
    granules = (depth * (2 * width // LANES) // 2, rows, LANES)
    copies = kernel(
        pack,
        jax.ShapeDtypeStruct((chips * groups, *granules), batch_own.dtype),
        (pltpu.VMEM(granules, batch_own.dtype),),
        limit=2,
    )(batch_own)
    batch_own = lax.all_to_all(copies, (X, Y), 0, 0, tiled=True)
    high, low, weights = kernel(
        lift,
        (
            jax.ShapeDtypeStruct((lines, count), jnp.bfloat16),
            jax.ShapeDtypeStruct((lines, count), jnp.bfloat16),
            array(vectors, count),
        ),
        (pltpu.VMEM((lines, count), jnp.float32),),
        limit=6,
    )(eigen_vectors, eigen_scale[None], subset_index[None], coefficients)
    batch_own, center_pieces, high, low, weights = lax.optimization_barrier(
        (batch_own, center_pieces, high, low, weights)
    )
    batch_own = batch_own.reshape(chips, groups, *granules)
    batch_other = from_others(batch_own, K)[1]

    labels = batch_labels.reshape(chips, 1, 2 * LANES)
    index = batch_index.reshape(chips, 1, 2 * LANES)

    products = kernel(kernel_products, array(chips, lines, LANES), limit=12, padded=padded)
    sent = from_others(products(batch_own, *center_pieces, high, low), K)[1]
    kept = products(batch_other, *center_pieces, high, low)
    own = kernel(add, array(chips, lines, LANES), limit=6)(kept, sent)

    own = scattered(own, X)
    own = scattered(own.reshape(depth, lines // depth, LANES), Z)
    own = gathered(own, Z).reshape(lines, LANES)
    copies, basis = kernel(
        part, (array(chips, padded, LANES), array(chips, split, LANES)), limit=4
    )(own)
    basis = from_others(basis, Y)
    predicted = lax.all_to_all(copies, X, 0, 0, tiled=True)
    predicted, basis = lax.optimization_barrier((predicted, basis))

    half = kernel(
        project, array(groups * split, padded), classes=classes, rows_each=rows
    )(predicted, *basis, labels)
    halves = from_others(half, K)[:2]
    codes = jax.ShapeDtypeStruct((chips, groups * split, padded), jnp.int16)
    copies = kernel(join, codes, limit=4, classes=classes)(
        *halves
    )
    projected = lax.all_to_all(copies, X, 0, 0, tiled=True).reshape(vectors, padded)

    late = from_others(predicted, K)[:2]
    output, updated = kernel(
        step_batch, (array(classes, batch), array(classes, count)), rows_each=rows
    )(*late, labels, index, coefficients)
    result = kernel(correct, array(classes, count))(updated, projected, weights)
    return (output, result)


def solution(mesh, shape=(16, 4, 2)):
    finer = Mesh(mesh.devices.reshape(*shape, mesh.shape["cls"]), (*ROWS, Y))
    placed = (P(ROWS, Y), P(Y, ROWS), P(ROWS, Y), P(), P(), P(ROWS), P(ROWS, None), P())

    return jax.shard_map(
        shards,
        mesh=finer,
        in_specs=placed,
        out_specs=(P(Y, None), P(Y, ROWS)),
        check_vma=False,
    )
```
